512 devices in a mesh: fine: 16 (over z, core), coarse: 8 (over y), comp: 4 (over x).
Axes of the slice: x: 4, y: 8, z: 8, core: 2. Of those that a mesh axis runs over, the one named last changes fastest.
Arguments:
- a_vals: bfloat16 [6144, 64, 448], P(('fine', 'coarse', 'comp')), may hold values from -0.25 to 0.25
- a_cols: int32 [6144, 7], P(('fine', 'coarse', 'comp')), may hold values from 0 to 75, as said below
- p_vals: bfloat16 [6144, 64, 256], P(('fine', 'coarse', 'comp')), may hold values from -1 to 1
- p_cols: int32 [6144, 4], P(('fine', 'coarse', 'comp')), may hold values from 0 to 7, as said below
- gp_cols: int32 [32768, 4], P(('fine', 'coarse', 'comp')), may hold values from 0 to 15, as said below
- send_list: int32 [32768], P(('fine', 'coarse', 'comp')), may hold values from 0 to 11
Outputs:
- coarse_op: float32 [16, 512, 4, 1024], P('fine', 'coarse', 'comp')
The draws below stay inside these ranges and needn't reach their ends.
Inputs may be any that keep to these rules, and one draw needn't show every extreme that they name: `a_cols`: A value e below 12 names local row e of the same device, a value 12 + s names ghost slot s; the first entry of each row is the row itself, and every ghost slot of a device is named by at least one entry of its rows. `p_cols`: the 4 entries of a row are distinct. `gp_cols`: the 4 entries of a row are distinct.
All inputs are finite; a program needn't handle non-finite values.
Results may differ from the reference program's by a relative error of at most 0.0029.
Values may be sent and summed in bfloat16 or wider, within the bound.
No kernel may reach another device: no remote copies, remote signals or barrier semaphores. Data moves between devices by JAX's collectives and lax.ppermute only.
A program may use at most 64 MiB of HBM per device.

```python
import jax
import jax.numpy as jnp
from jax import lax

B = 64
KA = 7
KP = 4
NC = 8
EXT = 8
G = 1
NBD = 12
NCW = 16
GDEV = 64
NB = 6144
NGHOST = 32768
N_FINE = 16
N_COARSE = 8
N_COMP = 4
DEVICES = 512


def draw_a_cols(key, part):
    head_key, tail_key = jax.random.split(key)
    entry_count = NBD * (KA - 1)
    device_keys = jax.random.split(head_key, DEVICES)
    orders = jax.vmap(lambda single_key: jax.random.permutation(single_key, entry_count))(device_keys)
    nearby = jax.random.randint(tail_key, (DEVICES, entry_count), 0, NBD)
    others = jnp.where(orders < GDEV, NBD + orders, nearby).astype(jnp.int32).reshape(DEVICES, NBD, KA - 1)
    itself = jnp.broadcast_to(jnp.arange(NBD, dtype=jnp.int32)[None, :, None], (DEVICES, NBD, 1))
    return jnp.concatenate([itself, others], axis=2).reshape(NB, KA)


def distinct_columns(key, row_count, pick_count, span_width):
    row_keys = jax.random.split(key, row_count)
    picked = jax.vmap(lambda single_key: jax.random.permutation(single_key, span_width)[:pick_count])(row_keys)
    return picked.astype(jnp.int32)


def draw_p_cols(key, part):
    return distinct_columns(jax.random.fold_in(key, 11), NB, KP, NC)


def draw_gp_cols(key, part):
    return distinct_columns(jax.random.fold_in(key, 23), NGHOST, KP, NCW)


def place_ends(values, key, smallest, largest):
    shape = values.shape
    place = [jax.random.randint(jax.random.fold_in(key, axis), (), 0, shape[axis]) for axis in range(len(shape))]
    values = values.at[tuple(place)].set(smallest)
    longest = shape.index(max(shape))
    place[longest] = (place[longest] + 1) % shape[longest]
    return values.at[tuple(place)].set(largest)


def block_levels(key, dims, cuts, least, top_value):
    level, own = 1.0, jax.random.fold_in(key, 6)
    for dim, blocks in cuts:
        draws = jnp.exp(jax.random.uniform(jax.random.fold_in(own, dim), (blocks,), jnp.float32, least / len(cuts), top_value / len(cuts)))
        level = level * jnp.repeat(draws, dims[dim] // blocks).reshape([-1 if axis == dim else 1 for axis in range(len(dims))])
    return level


def noise(stream_key, shape, scale, reach, pieces=(), held_as=jnp.bfloat16):
    drawn = scale * jax.random.normal(stream_key, shape, jnp.float32)
    if pieces:
        drawn = drawn * block_levels(stream_key, shape, pieces, -0.22, 0.18)
    return jnp.clip(drawn, -reach, reach).astype(held_as)


def setup_inputs(seed: int = 0) -> dict:
    arg_keys = jax.random.split(jax.random.key(seed), 7)
    return {
        "a_vals": noise(arg_keys[0], (NB, B, KA * B), (B * KA) ** -0.5, 0.25, ((0, 512),)),
        "a_cols": draw_a_cols(jax.random.fold_in(arg_keys[6], 71), 0),
        "p_vals": noise(arg_keys[2], (NB, B, KP * B), 0.17, 1.0, ((0, 512),)),
        "p_cols": draw_p_cols(jax.random.fold_in(arg_keys[6], 71), 0),
        "gp_cols": draw_gp_cols(jax.random.fold_in(arg_keys[6], 71), 0),
        "send_list": place_ends(jax.random.randint(arg_keys[5], (NGHOST,), 0, NBD), jax.random.fold_in(arg_keys[5], 1), 0, NBD - 1).astype(jnp.int32),
    }


def local_terms(a_rows, a_index, p_rows, p_index, ghosts, g_index):
    block_rows = a_rows.shape[0]
    block_size = a_rows.shape[1]
    pick_count = p_index.shape[1]
    link_count = a_index.shape[1]
    columns_all = NC + EXT
    sources = jnp.concatenate([p_rows, ghosts], axis=0)
    source_cols = jnp.concatenate([p_index, g_index], axis=0).astype(jnp.int32)
    fetched = jnp.take(sources, a_index, axis=0)
    fetched_cols = jnp.take(source_cols, a_index, axis=0)
    column_ids = jnp.arange(columns_all, dtype=jnp.int32)
    placing = (fetched_cols[:, :, :, None] == column_ids[None, None, None, :]).astype(jnp.float32)
    a_split = a_rows.reshape(block_rows, block_size, link_count, block_size)
    terms = jnp.einsum("riam,ramn->rain", a_split.astype(jnp.float32), fetched.astype(jnp.float32))
    terms = terms.reshape(block_rows, block_size, link_count, pick_count, block_size)
    applied = jnp.einsum("rakc,riakj->ricj", placing, terms, precision=lax.Precision.HIGHEST)
    prod_rows = applied.astype(jnp.bfloat16).reshape(block_rows * block_size, columns_all * block_size)
    own_rows = p_rows.reshape(block_rows, block_size, pick_count, block_size)
    owned_ids = jnp.arange(NC, dtype=jnp.int32)
    spread = jnp.zeros((block_rows, block_size, NC, block_size), jnp.bfloat16)
    for pick in range(pick_count):
        hits = p_index[:, pick, None] == owned_ids[None, :]
        spread = jnp.where(hits[:, None, :, None], own_rows[:, :, pick, None, :], spread)
    spread = spread.reshape(block_rows * block_size, NC * block_size)
    return spread, prod_rows


def contract(spread, prod_rows):
    return lax.dot_general(spread, prod_rows, (((0,), (0,)), ((), ())), preferred_element_type=jnp.float32)


def reference(a_vals, a_cols, p_vals, p_cols, gp_cols, send_list):
    fine_n, coarse_n, comp_n = N_FINE, N_COARSE, N_COMP
    a_all = a_vals.reshape(fine_n, coarse_n, comp_n, NBD, B, KA * B)
    p_all = p_vals.reshape(fine_n, coarse_n, comp_n, NBD, B, KP * B)
    ac_all = a_cols.reshape(fine_n, coarse_n, comp_n, NBD, KA)
    pc_all = p_cols.reshape(fine_n, coarse_n, comp_n, NBD, KP)
    gc_all = gp_cols.reshape(fine_n, coarse_n, comp_n, GDEV, KP)
    wanted = jnp.transpose(send_list.reshape(fine_n, coarse_n, comp_n, fine_n, comp_n, G), (3, 1, 4, 0, 2, 5))
    fine_src = jnp.arange(fine_n, dtype=jnp.int32)[:, None, None]
    comp_src = jnp.arange(comp_n, dtype=jnp.int32)[None, :, None]

    def device_term(fine_idx, coarse_idx, comp_idx):
        ghosts = p_all[fine_src, coarse_idx, comp_src, wanted[fine_idx, coarse_idx, comp_idx]].reshape(GDEV, B, KP * B)
        spread, prod_rows = local_terms(a_all[fine_idx, coarse_idx, comp_idx], ac_all[fine_idx, coarse_idx, comp_idx], p_all[fine_idx, coarse_idx, comp_idx], pc_all[fine_idx, coarse_idx, comp_idx], ghosts, gc_all[fine_idx, coarse_idx, comp_idx])
        return contract(spread, prod_rows)

    def subdomain(index):
        fine_idx = index // comp_n
        comp_idx = index % comp_n

        def add_term(total, coarse_idx):
            return total + device_term(fine_idx, coarse_idx, comp_idx), None

        total, _ = lax.scan(add_term, jnp.zeros((NC * B, NCW * B), jnp.float32), jnp.arange(coarse_n, dtype=jnp.int32))
        return total

    blocks = lax.map(subdomain, jnp.arange(fine_n * comp_n, dtype=jnp.int32))
    return jnp.transpose(blocks.reshape(fine_n, comp_n, NC * B, NCW * B), (0, 2, 1, 3))
```

```python
import jax
import jax.numpy as jnp
from jax import lax
from jax.experimental import pallas as pl
from jax.experimental.pallas import tpu as pltpu
from jax.sharding import PartitionSpec as P

NC = 8
EXT = 8
WIDTHS = (32, 32)

NT = (((1,), (1,)), ((), ()))
NN = (((1,), (0,)), ((), ()))
VMEM_LIMIT = 48 * 1024 * 1024


def starts_of(widths):
    return [sum(widths[:c]) for c in range(len(widths))]


def pack_kernel(widths, send_ref, p_ref, *outs):
    rows, size, _ = p_ref.shape
    count = len(widths)
    local, sent = outs[:count], outs[count:]
    flat = p_ref[...].reshape(rows * size, 4 * size)
    row = lax.broadcasted_iota(jnp.int32, (2 * size, 4 * size), 0)
    col = lax.broadcasted_iota(jnp.int32, (2 * size, 4 * size), 1)
    wanted = jnp.zeros_like(row)
    base = 0
    for w, start in zip(widths, starts_of(widths)):
        for h in range(2):
            inside = (row >= base) & (row < base + w)
            wanted = jnp.where(inside, 2 * h * size + start + row - base, wanted)
            base += w
    turned = []
    for l in range(2):
        pick = (col == wanted + l * size).astype(jnp.float32).astype(jnp.bfloat16)
        turned.append(lax.dot_general(pick, flat, NT, preferred_element_type=jnp.float32))
    lane = lax.broadcasted_iota(jnp.int32, (2 * size, 2 * size), 1)
    for u in range(rows // 2):
        low = turned[0][:, u * 2 * size : (u + 1) * 2 * size]
        high = turned[1][:, u * 2 * size : (u + 1) * 2 * size]
        first = jnp.where(lane < size, low, pltpu.roll(high, size, 1)).astype(jnp.bfloat16)
        second = jnp.where(lane < size, pltpu.roll(low, size, 1), high).astype(jnp.bfloat16)
        base = 0
        for c, w in enumerate(widths):
            local[c][2 * u] = first[base : base + 2 * w]
            local[c][2 * u + 1] = second[base : base + 2 * w]
            base += 2 * w
    for c in range(count):
        for s in range(sent[c].shape[0]):
            sent[c][s] = local[c][send_ref[s]]


def pack(widths, send_list, p_vals):
    rows, size, _ = p_vals.shape
    slots = send_list.shape[0]
    vmem = pl.BlockSpec(memory_space=pltpu.VMEM)
    shapes = [jax.ShapeDtypeStruct((rows, 2 * w, 2 * size), p_vals.dtype) for w in widths]
    shapes += [jax.ShapeDtypeStruct((slots, 2 * w, 2 * size), p_vals.dtype) for w in widths]
    outs = pl.pallas_call(
        lambda *refs: pack_kernel(widths, *refs),
        out_shape=shapes,
        in_specs=[pl.BlockSpec(memory_space=pltpu.SMEM), vmem],
        out_specs=[vmem] * len(shapes),
        compiler_params=pltpu.CompilerParams(vmem_limit_bytes=VMEM_LIMIT),
        name="pack",
    )(send_list, p_vals)
    return outs[: len(widths)], outs[len(widths) :]


def prepare_kernel(p_cols_ref, p_ref, a_ref, spread_ref, mixed_ref, stacked):
    rows, size, _ = p_ref.shape
    width = a_ref.shape[2]
    links = width // size
    flat = p_ref[...].reshape(rows * size, 4 * size)
    row = lax.broadcasted_iota(jnp.int32, (4 * size, 4 * size), 0)
    col = lax.broadcasted_iota(jnp.int32, (4 * size, 4 * size), 1)
    eye = (row == col).astype(jnp.float32).astype(jnp.bfloat16)
    turned = lax.dot_general(eye, flat, NT, preferred_element_type=jnp.float32).astype(jnp.bfloat16)
    spread_ref[...] = jnp.zeros_like(spread_ref)
    for r in range(rows):
        for k in range(4):
            start = pl.multiple_of(p_cols_ref[k, r] * size, size)
            spread_ref[pl.ds(start, size), r * size : (r + 1) * size] = turned[
                k * size : (k + 1) * size, r * size : (r + 1) * size
            ]
    for r in range(rows):
        for a in range(links):
            stacked[a * size : (a + 1) * size, r * size : (r + 1) * size] = a_ref[r, :, a * size : (a + 1) * size]
    row = lax.broadcasted_iota(jnp.int32, (width, width), 0)
    col = lax.broadcasted_iota(jnp.int32, (width, width), 1)
    pair = links * (row % size) + row // size
    pick = (col == pair).astype(jnp.float32).astype(jnp.bfloat16)
    keep = (col // size == pair // size).astype(jnp.float32).astype(jnp.bfloat16)
    moved = lax.dot_general(pick, stacked[...], NN, preferred_element_type=jnp.float32).astype(jnp.bfloat16)
    for r in range(rows):
        part = moved[:, r * size : (r + 1) * size]
        mixed_ref[r] = jnp.concatenate([part] * links, axis=1) * keep


def prepare(p_cols, p_vals, a_vals):
    rows, size, _ = p_vals.shape
    width = a_vals.shape[2]
    vmem = pl.BlockSpec(memory_space=pltpu.VMEM)
    return pl.pallas_call(
        prepare_kernel,
        out_shape=[
            jax.ShapeDtypeStruct((NC * size, rows * size), p_vals.dtype),
            jax.ShapeDtypeStruct((rows, width, width), p_vals.dtype),
        ],
        in_specs=[pl.BlockSpec(memory_space=pltpu.SMEM), vmem, vmem],
        out_specs=[vmem, vmem],
        scratch_shapes=[pltpu.VMEM((width, rows * size), jnp.bfloat16)],
        compiler_params=pltpu.CompilerParams(vmem_limit_bytes=VMEM_LIMIT),
        name="prepare",
    )(p_cols.T, p_vals, a_vals)


def product_kernel(a_cols_ref, p_cols_ref, g_cols_ref, mixed_ref, spread_ref, local_ref, ghost_ref, out_ref, sources, cols, picked, terms, prod, sems, *sums):
    rows, width, _ = mixed_ref.shape
    links = a_cols_ref.shape[0]
    size = width // links
    w = local_ref.shape[1] // 2
    slots = ghost_ref.shape[0]
    copies = [
        pltpu.make_async_copy(local_ref, sources.at[pl.ds(0, rows)], sems.at[0]),
        pltpu.make_async_copy(ghost_ref, sources.at[pl.ds(rows, slots)], sems.at[1]),
    ]
    for copy in copies:
        copy.start()
    for r in range(rows):
        sums[r][...] = jnp.zeros_like(sums[r])
    for k in range(4):
        for e in range(rows):
            cols[k, e] = p_cols_ref[k, e]
        for e in range(slots):
            cols[k, rows + e] = g_cols_ref[k, e]
    for copy in copies:
        copy.wait()
    for r in range(rows):
        for a in range(links):
            e = a_cols_ref[a, r]
            for k in range(4):
                h, l = divmod(k, 2)
                picked[r, k * w : (k + 1) * w, a * size : (a + 1) * size] = sources[
                    e, h * w : (h + 1) * w, l * size : (l + 1) * size
                ]
        terms[r] = lax.dot_general(picked[r], mixed_ref[r], NT, preferred_element_type=jnp.float32)
    for a in range(links):
        for k in range(4):
            for r in range(rows):
                start = pl.multiple_of(cols[k, a_cols_ref[a, r]] * w, w)
                here = pl.ds(start, w)
                sums[r][here, :] = sums[r][here, :] + terms[r, k * w : (k + 1) * w, a * size : (a + 1) * size]
    for r in range(rows):
        prod[:, r * size : (r + 1) * size] = sums[r][...].astype(jnp.bfloat16)
    out_ref[...] = lax.dot_general(
        spread_ref[...], prod[...], NT, preferred_element_type=jnp.float32
    ).astype(jnp.bfloat16)


def product(a_cols, p_cols, gp_cols, mixed, spread_rows, local, ghosts):
    rows, width, _ = mixed.shape
    slots, double, lanes = ghosts.shape
    size = lanes // 2
    wide = (NC + EXT) * (double // 2)
    vmem = pl.BlockSpec(memory_space=pltpu.VMEM)
    smem = pl.BlockSpec(memory_space=pltpu.SMEM)
    anywhere = pl.BlockSpec(memory_space=pl.ANY)
    return pl.pallas_call(
        product_kernel,
        out_shape=jax.ShapeDtypeStruct((NC * size, wide), jnp.bfloat16),
        in_specs=[smem, smem, smem, vmem, vmem, anywhere, anywhere],
        out_specs=vmem,
        scratch_shapes=[
            pltpu.VMEM((rows + slots, double, lanes), jnp.bfloat16),
            pltpu.SMEM((4, rows + slots), jnp.int32),
            pltpu.VMEM((rows, 2 * double, width), jnp.bfloat16),
            pltpu.VMEM((rows, 2 * double, width), jnp.float32),
            pltpu.VMEM((wide, rows * size), jnp.bfloat16),
            pltpu.SemaphoreType.DMA((2,)),
        ]
        + [pltpu.VMEM((wide, size), jnp.float32)] * rows,
        compiler_params=pltpu.CompilerParams(vmem_limit_bytes=VMEM_LIMIT),
        name="product",
    )(a_cols.T, p_cols.T, gp_cols.T, mixed, spread_rows, local, ghosts)


def total_kernel(widths, *refs):
    parts, out_ref = refs[:-1], refs[-1]
    size = out_ref.shape[0]
    for part, w, start in zip(parts, widths, starts_of(widths)):
        total = part[0].astype(jnp.float32)
        for c in range(1, part.shape[0]):
            total = total + part[c].astype(jnp.float32)
        for j in range(NC + EXT):
            out_ref[:, 0, j * size + start : j * size + start + w] = total[:, j * w : (j + 1) * w]


def total(widths, parts):
    size = parts[0].shape[1]
    vmem = pl.BlockSpec(memory_space=pltpu.VMEM)
    return pl.pallas_call(
        lambda *refs: total_kernel(widths, *refs),
        out_shape=jax.ShapeDtypeStruct((size, 1, (NC + EXT) * size), jnp.float32),
        in_specs=[vmem] * len(parts),
        out_specs=vmem,
        compiler_params=pltpu.CompilerParams(vmem_limit_bytes=VMEM_LIMIT),
        name="total",
    )(*parts)


def on_device(a_vals, a_cols, p_vals, p_cols, gp_cols, send_list):
    size = p_vals.shape[1]
    local, outgoing = pack(WIDTHS, send_list, p_vals)
    spread_rows, mixed = prepare(p_cols, p_vals, a_vals)
    parts = []
    for c in range(len(WIDTHS)):
        arrived = lax.all_to_all(outgoing[c], ("fine", "comp"), split_axis=0, concat_axis=0, tiled=True)
        partial = product(a_cols, p_cols, gp_cols, mixed, spread_rows, local[c], arrived)
        moved = lax.all_to_all(partial, "coarse", split_axis=0, concat_axis=0, tiled=True)
        parts.append(moved.reshape(NC, size, -1))
    owned = total(WIDTHS, parts)
    return owned.reshape((1, owned.shape[0], 1, owned.shape[2]))


def solution(mesh):
    placed = (
        P(("fine", "coarse", "comp"), None, None),
        P(("fine", "coarse", "comp"), None),
        P(("fine", "coarse", "comp"), None, None),
        P(("fine", "coarse", "comp"), None),
        P(("fine", "coarse", "comp"), None),
        P(("fine", "coarse", "comp")),
    )
    return jax.shard_map(
        on_device,
        mesh=mesh,
        in_specs=placed,
        out_specs=P("fine", "coarse", "comp", None),
        check_vma=False,
    )
```

```python
import jax
import jax.numpy as jnp
from jax import lax
from jax.experimental import pallas as pl
from jax.experimental.pallas import tpu as pltpu
from jax.sharding import PartitionSpec as P

NC = 8
EXT = 8
PICKS = 4

NT = (((1,), (1,)), ((), ()))
NN = (((1,), (0,)), ((), ()))
MIB = 1024 * 1024
VMEM = pl.BlockSpec(memory_space=pltpu.VMEM)
SMEM = pl.BlockSpec(memory_space=pltpu.SMEM)
HBM = pl.BlockSpec(memory_space=pltpu.HBM)


def in_hbm(array):
    return pltpu.with_memory_space_constraint(array, pltpu.HBM)


def one_hot(condition):
    return condition.astype(jnp.float32).astype(jnp.bfloat16)


def pack_kernel(send_hbm, p_hbm, local_ref, sent_hbm, send_ref, p_ref, sems):
    rows, size, _ = p_ref.shape
    copies = [pltpu.make_async_copy(p_hbm, p_ref, sems.at[0]), pltpu.make_async_copy(send_hbm, send_ref, sems.at[1])]
    for copy in copies:
        copy.start()
    row = lax.broadcasted_iota(jnp.int32, (2 * size, PICKS * size), 0)
    col = lax.broadcasted_iota(jnp.int32, (2 * size, PICKS * size), 1)
    block = 2 * (row // size) * size + row % size
    lane = lax.broadcasted_iota(jnp.int32, (2 * size, 2 * size), 1)
    for copy in copies:
        copy.wait()
    flat = p_ref[...].reshape(rows * size, PICKS * size)
    turned = [
        lax.dot_general(one_hot(col == block + l * size), flat, NT, preferred_element_type=jnp.float32) for l in range(2)
    ]
    for u in range(rows // 2):
        low = turned[0][:, u * 2 * size : (u + 1) * 2 * size]
        high = turned[1][:, u * 2 * size : (u + 1) * 2 * size]
        local_ref[2 * u] = jnp.where(lane < size, low, pltpu.roll(high, size, 1)).astype(jnp.bfloat16)
        local_ref[2 * u + 1] = jnp.where(lane < size, pltpu.roll(low, size, 1), high).astype(jnp.bfloat16)
    moves = [
        pltpu.make_async_copy(local_ref.at[send_ref[s]], sent_hbm.at[s], sems.at[2]) for s in range(sent_hbm.shape[0])
    ]
    for move in moves:
        move.start()
    pltpu.make_async_copy(sent_hbm, sent_hbm, sems.at[2]).wait()


def pack(send_list, p_vals):
    rows, size, _ = p_vals.shape
    slots = send_list.shape[0]
    return pl.pallas_call(
        pack_kernel,
        out_shape=[
            pltpu.HBM((rows, 2 * size, 2 * size), p_vals.dtype),
            pltpu.HBM((slots, 2 * size, 2 * size), p_vals.dtype),
        ],
        in_specs=[HBM, HBM],
        out_specs=[VMEM, HBM],
        scratch_shapes=[
            pltpu.SMEM((slots,), jnp.int32),
            pltpu.VMEM(p_vals.shape, p_vals.dtype),
            pltpu.SemaphoreType.DMA((3,)),
        ],
        compiler_params=pltpu.CompilerParams(vmem_limit_bytes=8 * MIB),
        name="pack",
    )(in_hbm(send_list), in_hbm(p_vals))


def prepare_kernel(a_cols_ref, p_cols_ref, g_cols_ref, p_ref, a_ref, spread_ref, mixed_ref, start_ref, stacked):
    rows, size, _ = p_ref.shape
    width = a_ref.shape[2]
    links = width // size
    slots = g_cols_ref.shape[1]
    for b in range(links):
        for r in range(rows):
            e = a_cols_ref[b, r]
            near = jnp.minimum(e, rows - 1)
            far = jnp.clip(e - rows, 0, slots - 1)
            for k in range(PICKS):
                start_ref[b, rows * k + r] = size * jnp.where(e < rows, p_cols_ref[k, near], g_cols_ref[k, far])
    flat = p_ref[...].reshape(rows * size, PICKS * size)
    row = lax.broadcasted_iota(jnp.int32, (PICKS * size, PICKS * size), 0)
    col = lax.broadcasted_iota(jnp.int32, (PICKS * size, PICKS * size), 1)
    turned = lax.dot_general(one_hot(row == col), flat, NT, preferred_element_type=jnp.float32).astype(jnp.bfloat16)
    spread_ref[...] = jnp.zeros_like(spread_ref)
    for r in range(rows):
        for k in range(PICKS):
            start = pl.multiple_of(p_cols_ref[k, r] * size, size)
            spread_ref[pl.ds(start, size), r * size : (r + 1) * size] = turned[
                k * size : (k + 1) * size, r * size : (r + 1) * size
            ]
    for r in range(rows):
        for a in range(links):
            stacked[a * size : (a + 1) * size, r * size : (r + 1) * size] = a_ref[r, :, a * size : (a + 1) * size]
    row = lax.broadcasted_iota(jnp.int32, (width, width), 0)
    col = lax.broadcasted_iota(jnp.int32, (width, width), 1)
    pair = links * (row % size) + row // size
    moved = lax.dot_general(one_hot(col == pair), stacked[...], NN, preferred_element_type=jnp.float32).astype(jnp.bfloat16)
    for r in range(rows):
        part = moved[:, r * size : (r + 1) * size]
        mixed_ref[r] = jnp.concatenate([part, part], axis=1)


def prepare(a_cols, p_cols, gp_cols, p_vals, a_vals):
    rows, size, _ = p_vals.shape
    width = a_vals.shape[2]
    links = width // size
    return pl.pallas_call(
        prepare_kernel,
        out_shape=[
            pltpu.HBM((NC * size, rows * size), p_vals.dtype),
            pltpu.HBM((rows, width, 2 * size), p_vals.dtype),
            jax.ShapeDtypeStruct((links, PICKS * rows), jnp.int32),
        ],
        in_specs=[SMEM, SMEM, SMEM, VMEM, VMEM],
        out_specs=[VMEM, VMEM, SMEM],
        scratch_shapes=[pltpu.VMEM((width, rows * size), jnp.bfloat16)],
        compiler_params=pltpu.CompilerParams(vmem_limit_bytes=20 * MIB),
        name="prepare",
    )(a_cols.T, p_cols.T, gp_cols.T, p_vals, a_vals)


def product_kernel(a_cols_ref, start_ref, mixed_hbm, spread_hbm, local_hbm, ghost_ref, out_ref, mixed_ref, spread_ref, local_ref, placed, picked, terms, prod, sems, *sums):
    rows, width, double = mixed_ref.shape
    size = double // 2
    links = width // size
    slots = ghost_ref.shape[0]
    copies = [
        pltpu.make_async_copy(local_hbm, local_ref, sems.at[0]),
        pltpu.make_async_copy(mixed_hbm, mixed_ref, sems.at[1]),
        pltpu.make_async_copy(spread_hbm, spread_ref, sems.at[2]),
    ]
    for copy in copies:
        copy.start()
    for total in sums:
        total[...] = jnp.zeros_like(total)
    row = lax.broadcasted_iota(jnp.int32, (width, width), 0)
    col = lax.broadcasted_iota(jnp.int32, (width, width), 1)
    keep = one_hot(col // size == (links * (row % size) + row // size) // size)
    copies[0].wait()
    copies[1].wait()
    for r in range(rows):
        for a in range(links):
            e = a_cols_ref[a, r]
            near = local_ref[jnp.minimum(e, rows - 1)]
            far = ghost_ref[jnp.clip(e - rows, 0, slots - 1)]
            source = jnp.where(e < rows, near, far)
            for k in range(PICKS):
                h, l = divmod(k, 2)
                picked[r, k * size : (k + 1) * size, a * size : (a + 1) * size] = source[
                    h * size : (h + 1) * size, l * size : (l + 1) * size
                ]
        twice = mixed_ref[r]
        for t in range(0, width, double):
            stop = min(t + double, width)
            placed[r, :, t:stop] = twice[:, : stop - t] * keep[:, t:stop]
        terms[r] = lax.dot_general(picked[r], placed[r], NT, preferred_element_type=jnp.float32)
    for b in range(links):
        for k in range(PICKS):
            for odd in range(2):
                for u in range(rows // 2):
                    r = 2 * u + odd
                    here = pl.ds(pl.multiple_of(start_ref[b, rows * k + r], size), size)
                    lanes = slice(odd * size, (odd + 1) * size)
                    sums[u][here, lanes] = (
                        sums[u][here, lanes] + terms[r, k * size : (k + 1) * size, b * size : (b + 1) * size]
                    )
    for u in range(rows // 2):
        prod[:, 2 * u * size : 2 * (u + 1) * size] = sums[u][...].astype(jnp.bfloat16)
    copies[2].wait()
    out_ref[...] = lax.dot_general(
        spread_ref[...], prod[...], NT, preferred_element_type=jnp.float32
    ).astype(jnp.bfloat16)


def product(a_cols, start, mixed, spread, local, ghosts):
    rows, width, _ = mixed.shape
    size = local.shape[1] // 2
    wide = (NC + EXT) * size
    return pl.pallas_call(
        product_kernel,
        out_shape=jax.ShapeDtypeStruct((NC * size, wide), jnp.bfloat16),
        in_specs=[SMEM, SMEM, HBM, HBM, HBM, VMEM],
        out_specs=VMEM,
        scratch_shapes=[
            pltpu.VMEM(mixed.shape, jnp.bfloat16),
            pltpu.VMEM(spread.shape, jnp.bfloat16),
            pltpu.VMEM(local.shape, jnp.bfloat16),
            pltpu.VMEM((rows, width, width), jnp.bfloat16),
            pltpu.VMEM((rows, PICKS * size, width), jnp.bfloat16),
            pltpu.VMEM((rows, PICKS * size, width), jnp.float32),
            pltpu.VMEM((wide, rows * size), jnp.bfloat16),
            pltpu.SemaphoreType.DMA((3,)),
        ]
        + [pltpu.VMEM((wide, 2 * size), jnp.float32)] * (rows // 2),
        compiler_params=pltpu.CompilerParams(vmem_limit_bytes=32 * MIB),
        name="product",
    )(a_cols.T, start, in_hbm(mixed), in_hbm(spread), in_hbm(local), ghosts)


def total_kernel(part_ref, out_ref):
    total = part_ref[0].astype(jnp.float32)
    for c in range(1, part_ref.shape[0]):
        total = total + part_ref[c].astype(jnp.float32)
    out_ref[:, 0, :] = total


def total(parts):
    _, size, wide = parts.shape
    return pl.pallas_call(
        total_kernel,
        out_shape=jax.ShapeDtypeStruct((size, 1, wide), jnp.float32),
        in_specs=[VMEM],
        out_specs=VMEM,
        compiler_params=pltpu.CompilerParams(vmem_limit_bytes=8 * MIB),
        name="total",
    )(parts)


def on_device(a_vals, a_cols, p_vals, p_cols, gp_cols, send_list):
    size = p_vals.shape[1]
    local, outgoing = pack(send_list, p_vals)
    arrived = lax.all_to_all(outgoing, ("fine", "comp"), split_axis=0, concat_axis=0, tiled=True)
    spread, mixed, start = prepare(a_cols, p_cols, gp_cols, p_vals, a_vals)
    partial = product(a_cols, start, mixed, spread, local, arrived)
    moved = lax.all_to_all(partial, "coarse", split_axis=0, concat_axis=0, tiled=True)
    owned = total(moved.reshape(NC, size, -1))
    return owned.reshape((1, owned.shape[0], 1, owned.shape[2]))


def solution(mesh):
    placed = (
        P(("fine", "coarse", "comp"), None, None),
        P(("fine", "coarse", "comp"), None),
        P(("fine", "coarse", "comp"), None, None),
        P(("fine", "coarse", "comp"), None),
        P(("fine", "coarse", "comp"), None),
        P(("fine", "coarse", "comp")),
    )
    return jax.shard_map(
        on_device,
        mesh=mesh,
        in_specs=placed,
        out_specs=P("fine", "coarse", "comp", None),
        check_vma=False,
    )
```

```python
import jax
import jax.numpy as jnp
from jax import lax
from jax.experimental import pallas as pl
from jax.experimental.pallas import tpu as pltpu
from jax.sharding import Mesh
from jax.sharding import PartitionSpec as P

NC = 8
EXT = 8
PICKS = 4

NT = (((1,), (1,)), ((), ()))
NN = (((1,), (0,)), ((), ()))
MIB = 1024 * 1024
VMEM = pl.BlockSpec(memory_space=pltpu.VMEM)
SMEM = pl.BlockSpec(memory_space=pltpu.SMEM)
HBM = pl.BlockSpec(memory_space=pltpu.HBM)


def in_hbm(array):
    return pltpu.with_memory_space_constraint(array, pltpu.HBM)


def one_hot(condition):
    return condition.astype(jnp.float32).astype(jnp.bfloat16)


def pack_kernel(send_hbm, p_hbm, sent_hbm, send_ref, p_ref, packed_ref, sems):
    rows, size, _ = p_ref.shape
    w = size // 2
    copies = [pltpu.make_async_copy(p_hbm, p_ref, sems.at[0]), pltpu.make_async_copy(send_hbm, send_ref, sems.at[1])]
    for copy in copies:
        copy.start()
    row = lax.broadcasted_iota(jnp.int32, (2 * size, PICKS * size), 0)
    col = lax.broadcasted_iota(jnp.int32, (2 * size, PICKS * size), 1)
    block = 2 * (row % size // w) * size + row // size * w + row % w
    lane = lax.broadcasted_iota(jnp.int32, (2 * size, 2 * size), 1)
    picks = [one_hot(col == block + l * size) for l in range(2)]
    for copy in copies:
        copy.wait()
    flat = p_ref[...].reshape(rows * size, PICKS * size)
    turned = [lax.dot_general(pick, flat, NT, preferred_element_type=jnp.float32) for pick in picks]
    for u in range(rows // 2):
        low = turned[0][:, u * 2 * size : (u + 1) * 2 * size]
        high = turned[1][:, u * 2 * size : (u + 1) * 2 * size]
        even = jnp.where(lane < size, low, pltpu.roll(high, size, 1)).astype(jnp.bfloat16)
        odd = jnp.where(lane < size, pltpu.roll(low, size, 1), high).astype(jnp.bfloat16)
        for d in range(2):
            packed_ref[2 * u, d] = even[d * size : (d + 1) * size]
            packed_ref[2 * u + 1, d] = odd[d * size : (d + 1) * size]
    moves = []
    for f in range(sent_hbm.shape[0]):
        for m in range(sent_hbm.shape[2]):
            slot = f * sent_hbm.shape[2] + m
            moves.append(pltpu.make_async_copy(packed_ref.at[send_ref[slot]], sent_hbm.at[f, :, m], sems.at[2]))
    for move in moves:
        move.start()
    pltpu.make_async_copy(sent_hbm, sent_hbm, sems.at[2]).wait()


def pack(send_list, p_vals, comp):
    rows, size, _ = p_vals.shape
    slots = send_list.shape[0]
    return pl.pallas_call(
        pack_kernel,
        out_shape=pltpu.HBM((slots // comp, 2, comp, size, 2 * size), p_vals.dtype),
        in_specs=[HBM, HBM],
        out_specs=HBM,
        scratch_shapes=[
            pltpu.SMEM((slots,), jnp.int32),
            pltpu.VMEM(p_vals.shape, p_vals.dtype),
            pltpu.VMEM((rows, 2, size, 2 * size), p_vals.dtype),
            pltpu.SemaphoreType.DMA((3,)),
        ],
        compiler_params=pltpu.CompilerParams(vmem_limit_bytes=8 * MIB),
        name="pack",
    )(in_hbm(send_list), in_hbm(p_vals))


def prepare_kernel(links, comp, where_ref, tables_ref, p_ref, a_ref, spread_ref, mixed_ref, local_ref, start_ref, source_ref, stacked):
    rows, size, _ = p_ref.shape
    width = a_ref.shape[2]
    w = size // 2
    slots = tables_ref.shape[1]
    half = where_ref[0]
    place = where_ref[1]
    for b in range(links):
        for r in range(rows):
            e = tables_ref[b, r]
            near = jnp.minimum(e, rows - 1)
            far = jnp.clip(e - rows, 0, slots - 1)
            arrived = rows + (2 * (far // comp) + place) * comp + far % comp
            source_ref[b, r] = jnp.where(e < rows, near, arrived)
            for k in range(PICKS):
                c = jnp.where(e < rows, tables_ref[links + k, near], tables_ref[links + PICKS + k, far])
                spot = c // 4 * 4 + c % 2 * 2 + jnp.where(half == 0, c // 2 % 2, 1 - c // 2 % 2)
                start_ref[b, rows * k + r] = spot * w
    flat = p_ref[...].reshape(rows * size, PICKS * size)
    row = lax.broadcasted_iota(jnp.int32, (PICKS * size, PICKS * size), 0)
    col = lax.broadcasted_iota(jnp.int32, (PICKS * size, PICKS * size), 1)
    turned = lax.dot_general(one_hot(row == col), flat, NT, preferred_element_type=jnp.float32).astype(jnp.bfloat16)
    spread_ref[...] = jnp.zeros_like(spread_ref)
    for r in range(rows):
        for k in range(PICKS):
            start = pl.multiple_of(tables_ref[links + k, r] * size, size)
            spread_ref[pl.ds(start, size), r * size : (r + 1) * size] = turned[
                k * size : (k + 1) * size, r * size : (r + 1) * size
            ]
    row = lax.broadcasted_iota(jnp.int32, (size, PICKS * size), 0)
    col = lax.broadcasted_iota(jnp.int32, (size, PICKS * size), 1)
    block = 2 * (row // w) * size + half * w + row % w
    lane = lax.broadcasted_iota(jnp.int32, (size, 2 * size), 1)
    packed = [
        lax.dot_general(one_hot(col == block + l * size), flat, NT, preferred_element_type=jnp.float32) for l in range(2)
    ]
    for u in range(rows // 2):
        low = packed[0][:, u * 2 * size : (u + 1) * 2 * size]
        high = packed[1][:, u * 2 * size : (u + 1) * 2 * size]
        local_ref[2 * u] = jnp.where(lane < size, low, pltpu.roll(high, size, 1)).astype(jnp.bfloat16)
        local_ref[2 * u + 1] = jnp.where(lane < size, pltpu.roll(low, size, 1), high).astype(jnp.bfloat16)
    for r in range(rows):
        for a in range(links):
            stacked[a * size : (a + 1) * size, r * size : (r + 1) * size] = a_ref[r, :, a * size : (a + 1) * size]
    row = lax.broadcasted_iota(jnp.int32, (width, width), 0)
    col = lax.broadcasted_iota(jnp.int32, (width, width), 1)
    pair = links * (row % size) + row // size
    moved = lax.dot_general(one_hot(col == pair), stacked[...], NN, preferred_element_type=jnp.float32).astype(jnp.bfloat16)
    for r in range(rows):
        part = moved[:, r * size : (r + 1) * size]
        mixed_ref[r] = jnp.concatenate([part, part], axis=1)


def prepare(comp, where, tables, p_vals, a_vals):
    rows, size, _ = p_vals.shape
    width = a_vals.shape[2]
    links = width // size
    return pl.pallas_call(
        lambda *refs: prepare_kernel(links, comp, *refs),
        out_shape=[
            pltpu.HBM((NC * size, rows * size), p_vals.dtype),
            pltpu.HBM((rows, width, 2 * size), p_vals.dtype),
            pltpu.HBM((rows, size, 2 * size), p_vals.dtype),
            jax.ShapeDtypeStruct((links, PICKS * rows), jnp.int32),
            jax.ShapeDtypeStruct((links, rows), jnp.int32),
        ],
        in_specs=[SMEM, SMEM, VMEM, VMEM],
        out_specs=[VMEM, VMEM, VMEM, SMEM, SMEM],
        scratch_shapes=[pltpu.VMEM((width, rows * size), jnp.bfloat16)],
        compiler_params=pltpu.CompilerParams(vmem_limit_bytes=20 * MIB),
        name="prepare",
    )(where, tables, p_vals, a_vals)


def product_kernel(*refs):
    starts, sources, spreads_hbm, mixed_hbm, local_hbm = (refs[i : i + 2] for i in range(0, 10, 2))
    ghost_ref, out_ref, spread_ref, mixed_ref, local_ref, placed, picked, terms, prod, sems = refs[10:20]
    sums = refs[20:]
    _, rows, width, double = mixed_ref.shape
    size = double // 2
    w = size // 2
    links = width // size
    slots = ghost_ref.shape[0]
    copies = []
    for n, (here, there) in enumerate(((local_hbm, local_ref), (mixed_hbm, mixed_ref), (spreads_hbm, spread_ref))):
        for o in range(2):
            copies.append(pltpu.make_async_copy(here[o], there.at[o], sems.at[2 * n + o]))
    for copy in copies:
        copy.start()
    for total in sums:
        total[...] = jnp.zeros_like(total)
    row = lax.broadcasted_iota(jnp.int32, (width, width), 0)
    col = lax.broadcasted_iota(jnp.int32, (width, width), 1)
    keep = one_hot(col // size == (links * (row % size) + row // size) // size)
    for copy in copies[:4]:
        copy.wait()
    for o in range(2):
        for r in range(rows):
            q = o * rows + r
            for a in range(links):
                e = sources[o][a, r]
                near = local_ref[o, jnp.minimum(e, rows - 1)]
                far = ghost_ref[jnp.clip(e - rows, 0, slots - 1)]
                source = jnp.where(e < rows, near, far)
                for k in range(PICKS):
                    h, l = divmod(k, 2)
                    picked[q, k * w : (k + 1) * w, a * size : (a + 1) * size] = source[
                        h * w : (h + 1) * w, l * size : (l + 1) * size
                    ]
            twice = mixed_ref[o, r]
            for t in range(0, width, double):
                stop = min(t + double, width)
                placed[q, :, t:stop] = twice[:, : stop - t] * keep[:, t:stop]
            terms[q] = lax.dot_general(picked[q], placed[q], NT, preferred_element_type=jnp.float32)
    for b in range(links):
        for k in range(PICKS):
            for odd in range(2):
                for u in range(rows):
                    o, r = divmod(2 * u + odd, rows)
                    here = pl.ds(pl.multiple_of(starts[o][b, rows * k + r], w), w)
                    lanes = slice(odd * size, (odd + 1) * size)
                    sums[u][here, lanes] = (
                        sums[u][here, lanes] + terms[2 * u + odd, k * w : (k + 1) * w, b * size : (b + 1) * size]
                    )
    for u in range(rows):
        prod[:, u * double : (u + 1) * double] = sums[u][...].astype(jnp.bfloat16)
    for copy in copies[4:]:
        copy.wait()
    whole = rows * size
    out_ref[...] = (
        lax.dot_general(spread_ref[0], prod[:, :whole], NT, preferred_element_type=jnp.float32)
        + lax.dot_general(spread_ref[1], prod[:, whole:], NT, preferred_element_type=jnp.float32)
    ).astype(jnp.bfloat16)


def product(mine, other, ghosts):
    spread, mixed, local, _, _ = mine
    rows, width, double = mixed.shape
    size = double // 2
    wide = (NC + EXT) * (size // 2)
    operands = []
    for n in (3, 4):
        operands += [mine[n], other[n]]
    for n in (0, 1, 2):
        operands += [in_hbm(mine[n]), in_hbm(other[n])]
    return pl.pallas_call(
        product_kernel,
        out_shape=jax.ShapeDtypeStruct((NC * size, wide), jnp.bfloat16),
        in_specs=[SMEM] * 4 + [HBM] * 6 + [VMEM],
        out_specs=VMEM,
        scratch_shapes=[
            pltpu.VMEM((2, *spread.shape), jnp.bfloat16),
            pltpu.VMEM((2, *mixed.shape), jnp.bfloat16),
            pltpu.VMEM((2, *local.shape), jnp.bfloat16),
            pltpu.VMEM((2 * rows, width, width), jnp.bfloat16),
            pltpu.VMEM((2 * rows, 2 * size, width), jnp.bfloat16),
            pltpu.VMEM((2 * rows, 2 * size, width), jnp.float32),
            pltpu.VMEM((wide, 2 * rows * size), jnp.bfloat16),
            pltpu.SemaphoreType.DMA((6,)),
        ]
        + [pltpu.VMEM((wide, double), jnp.float32)] * rows,
        compiler_params=pltpu.CompilerParams(vmem_limit_bytes=44 * MIB),
        name="product",
    )(*operands, ghosts)


def total_kernel(part_ref, out_ref):
    parts, size, wide = part_ref.shape
    halves = []
    for d in range(2):
        total = part_ref[d].astype(jnp.float32)
        for c in range(d + 2, parts, 2):
            total = total + part_ref[c].astype(jnp.float32)
        halves.append(total)
    group = 2 * size
    first = lax.broadcasted_iota(jnp.int32, (size, group), 1) // (size // 2) % 2 == 0
    for u in range(wide // group):
        low = halves[0][:, u * group : (u + 1) * group]
        high = halves[1][:, u * group : (u + 1) * group]
        out_ref[:, 0, 2 * u * group : (2 * u + 1) * group] = jnp.where(first, low, high)
        out_ref[:, 0, (2 * u + 1) * group : (2 * u + 2) * group] = jnp.where(
            first, pltpu.roll(low, group - size // 2, 1), pltpu.roll(high, size // 2, 1)
        )


def total(parts):
    _, size, wide = parts.shape
    return pl.pallas_call(
        total_kernel,
        out_shape=jax.ShapeDtypeStruct((size, 1, 2 * wide), jnp.float32),
        in_specs=[VMEM],
        out_specs=VMEM,
        compiler_params=pltpu.CompilerParams(vmem_limit_bytes=8 * MIB),
        name="total",
    )(parts)


def on_device(a_vals, a_cols, p_vals, p_cols, gp_cols, send_list):
    size = p_vals.shape[1]
    slots = send_list.shape[0]
    comp = lax.axis_size("comp")
    outgoing = pack(send_list, p_vals, comp)
    outgoing = outgoing.reshape(-1, *outgoing.shape[3:])
    arrived = lax.all_to_all(outgoing, ("fine", "inner", "comp"), split_axis=0, concat_axis=0, tiled=True)
    half = lax.axis_index("inner")
    columns = [jnp.pad(table.T, ((0, 0), (0, slots - table.shape[0]))) for table in (a_cols, p_cols, gp_cols)]
    tables = jnp.concatenate(columns, axis=0)
    swap = ((0, 1), (1, 0))
    a_other, p_other, tables_other = (lax.ppermute(array, "inner", swap) for array in (a_vals, p_vals, tables))
    mine = prepare(comp, jnp.stack([half, half]), tables, p_vals, a_vals)
    other = prepare(comp, jnp.stack([half, 1 - half]), tables_other, p_other, a_other)
    partial = product(mine, other, arrived)
    moved = lax.all_to_all(partial, ("outer", "inner"), split_axis=0, concat_axis=0, tiled=True)
    owned = total(moved.reshape(NC, size, -1))
    return owned.reshape((1, owned.shape[0], 1, owned.shape[2]))


def solution(mesh):
    fine, coarse, comp = mesh.devices.shape
    pairs = Mesh(mesh.devices.reshape(fine, coarse // 2, 2, comp), ("fine", "outer", "inner", "comp"))
    rows = ("fine", "outer", "inner", "comp")
    placed = (
        P(rows, None, None),
        P(rows, None),
        P(rows, None, None),
        P(rows, None),
        P(rows, None),
        P(rows),
    )
    return jax.shard_map(
        on_device,
        mesh=pairs,
        in_specs=placed,
        out_specs=P("fine", ("outer", "inner"), "comp", None),
        check_vma=False,
    )
```

```python
import jax
import jax.numpy as jnp
from jax import lax
from jax.experimental import pallas as pl
from jax.experimental.pallas import tpu as pltpu
from jax.sharding import Mesh
from jax.sharding import PartitionSpec as P

NC = 8
EXT = 8
PICKS = 4

NT = (((1,), (1,)), ((), ()))
NN = (((1,), (0,)), ((), ()))
MIB = 1024 * 1024
VMEM = pl.BlockSpec(memory_space=pltpu.VMEM)
SMEM = pl.BlockSpec(memory_space=pltpu.SMEM)
HBM = pl.BlockSpec(memory_space=pltpu.HBM)


def in_hbm(array):
    return pltpu.with_memory_space_constraint(array, pltpu.HBM)


def one_hot(condition):
    return condition.astype(jnp.float32).astype(jnp.bfloat16)


def pack_kernel(send_hbm, p_hbm, sent_hbm, send_ref, p_ref, packed_ref, sems):
    rows, size, _ = p_ref.shape
    w = size // 2
    copies = [pltpu.make_async_copy(p_hbm, p_ref, sems.at[0]), pltpu.make_async_copy(send_hbm, send_ref, sems.at[1])]
    for copy in copies:
        copy.start()
    row = lax.broadcasted_iota(jnp.int32, (2 * size, PICKS * size), 0)
    col = lax.broadcasted_iota(jnp.int32, (2 * size, PICKS * size), 1)
    block = 2 * (row % size // w) * size + row // size * w + row % w
    lane = lax.broadcasted_iota(jnp.int32, (2 * size, 2 * size), 1)
    picks = [one_hot(col == block + l * size) for l in range(2)]
    for copy in copies:
        copy.wait()
    flat = p_ref[...].reshape(rows * size, PICKS * size)
    turned = [lax.dot_general(pick, flat, NT, preferred_element_type=jnp.float32) for pick in picks]
    for u in range(rows // 2):
        low = turned[0][:, u * 2 * size : (u + 1) * 2 * size]
        high = turned[1][:, u * 2 * size : (u + 1) * 2 * size]
        even = jnp.where(lane < size, low, pltpu.roll(high, size, 1)).astype(jnp.bfloat16)
        odd = jnp.where(lane < size, pltpu.roll(low, size, 1), high).astype(jnp.bfloat16)
        for d in range(2):
            packed_ref[2 * u, d] = even[d * size : (d + 1) * size]
            packed_ref[2 * u + 1, d] = odd[d * size : (d + 1) * size]
    moves = []
    for f in range(sent_hbm.shape[0]):
        for m in range(sent_hbm.shape[2]):
            slot = f * sent_hbm.shape[2] + m
            moves.append(pltpu.make_async_copy(packed_ref.at[send_ref[slot]], sent_hbm.at[f, :, m], sems.at[2]))
    for move in moves:
        move.start()
    pltpu.make_async_copy(sent_hbm, sent_hbm, sems.at[2]).wait()


def pack(send_list, p_vals, comp):
    rows, size, _ = p_vals.shape
    slots = send_list.shape[0]
    return pl.pallas_call(
        pack_kernel,
        out_shape=pltpu.HBM((slots // comp, 2, comp, size, 2 * size), p_vals.dtype),
        in_specs=[HBM, HBM],
        out_specs=HBM,
        scratch_shapes=[
            pltpu.SMEM((slots,), jnp.int32),
            pltpu.VMEM(p_vals.shape, p_vals.dtype),
            pltpu.VMEM((rows, 2, size, 2 * size), p_vals.dtype),
            pltpu.SemaphoreType.DMA((3,)),
        ],
        compiler_params=pltpu.CompilerParams(vmem_limit_bytes=8 * MIB),
        name="pack",
    )(in_hbm(send_list), in_hbm(p_vals))


def index_kernel(links, comp, place_ref, tables_ref, mine_ref, other_ref):
    rows = 3 * PICKS
    size = tables_ref.shape[1]
    w = size // 2
    place = place_ref[0]
    shift = comp.bit_length() - 1
    for b in range(links):
        for r in range(rows):
            e = tables_ref[b, r]
            is_local = e < rows
            near = jnp.minimum(e, rows - 1)
            far = jnp.clip(e - rows, 0, size - 1)
            slot = ((far >> shift) << (shift + 1)) + (place << shift) + (far & (comp - 1))
            source = jnp.where(is_local, near, rows + slot)
            mine_ref[b, PICKS * rows + r] = source
            other_ref[b, PICKS * rows + r] = source
            for k in range(PICKS):
                c = jnp.where(is_local, tables_ref[links + k, near], tables_ref[links + PICKS + k, far])
                base = (c & 12) + ((c & 1) << 1)
                upper = (c >> 1) & 1
                mine_ref[b, rows * k + r] = w * (base + (upper ^ place))
                other_ref[b, rows * k + r] = w * (base + (upper ^ place ^ 1))
    for k in range(PICKS):
        for r in range(rows):
            mine_ref[k, size + r] = tables_ref[links + k, r]
            other_ref[k, size + r] = tables_ref[links + k, r]


def index(links, comp, place, tables):
    assert comp & (comp - 1) == 0
    shape = jax.ShapeDtypeStruct((links, 2 * tables.shape[1]), jnp.int32)
    return pl.pallas_call(
        lambda *refs: index_kernel(links, comp, *refs),
        out_shape=[shape, shape],
        in_specs=[SMEM, SMEM],
        out_specs=[SMEM, SMEM],
        name="index",
    )(place, tables)


def layout_kernel(half_ref, table_ref, p_ref, spread_ref, local_ref):
    rows, size, _ = p_ref.shape
    w = size // 2
    half = half_ref[0]
    spread_ref[...] = jnp.zeros_like(spread_ref)
    flat = p_ref[...].reshape(rows * size, PICKS * size)
    row = lax.broadcasted_iota(jnp.int32, (PICKS * size, PICKS * size), 0)
    col = lax.broadcasted_iota(jnp.int32, (PICKS * size, PICKS * size), 1)
    turned = lax.dot_general(one_hot(row == col), flat, NT, preferred_element_type=jnp.float32)
    for r in range(rows):
        for k in range(PICKS):
            start = pl.multiple_of(table_ref[k, size + r] * size, size)
            spread_ref[pl.ds(start, size), r * size : (r + 1) * size] = turned[
                k * size : (k + 1) * size, r * size : (r + 1) * size
            ].astype(jnp.bfloat16)
    row = lax.broadcasted_iota(jnp.int32, (size, PICKS * size), 0)
    col = lax.broadcasted_iota(jnp.int32, (size, PICKS * size), 1)
    block = 2 * size * jnp.where(row < w, 0, 1) + half * w + jnp.where(row < w, row, row - w)
    lane = lax.broadcasted_iota(jnp.int32, (size, 2 * size), 1)
    packed = [
        lax.dot_general(one_hot(col == block + l * size), flat, NT, preferred_element_type=jnp.float32) for l in range(2)
    ]
    for u in range(rows // 2):
        low = packed[0][:, u * 2 * size : (u + 1) * 2 * size]
        high = packed[1][:, u * 2 * size : (u + 1) * 2 * size]
        local_ref[2 * u] = jnp.where(lane < size, low, pltpu.roll(high, size, 1)).astype(jnp.bfloat16)
        local_ref[2 * u + 1] = jnp.where(lane < size, pltpu.roll(low, size, 1), high).astype(jnp.bfloat16)


def layout(half, table, p_vals):
    rows, size, _ = p_vals.shape
    return pl.pallas_call(
        layout_kernel,
        out_shape=[
            pltpu.HBM((NC * size, rows * size), p_vals.dtype),
            pltpu.HBM((rows, size, 2 * size), p_vals.dtype),
        ],
        in_specs=[SMEM, SMEM, VMEM],
        out_specs=[VMEM, VMEM],
        compiler_params=pltpu.CompilerParams(vmem_limit_bytes=12 * MIB),
        name="layout",
    )(half, table, p_vals)


def regroup_kernel(a_ref, mixed_ref, stacked):
    rows, size, width = a_ref.shape
    links = width // size
    row = lax.broadcasted_iota(jnp.int32, (width, width), 0)
    col = lax.broadcasted_iota(jnp.int32, (width, width), 1)
    pair = links * (row & (size - 1)) + row // size
    for r in range(rows):
        for a in range(links):
            stacked[a * size : (a + 1) * size, r * size : (r + 1) * size] = a_ref[r, :, a * size : (a + 1) * size]
    moved = lax.dot_general(one_hot(col == pair), stacked[...], NN, preferred_element_type=jnp.float32).astype(jnp.bfloat16)
    for r in range(rows):
        part = moved[:, r * size : (r + 1) * size]
        mixed_ref[r] = jnp.concatenate([part, part], axis=1)


def regroup(a_vals):
    rows, size, width = a_vals.shape
    return pl.pallas_call(
        regroup_kernel,
        out_shape=pltpu.HBM((rows, width, 2 * size), a_vals.dtype),
        in_specs=[VMEM],
        out_specs=VMEM,
        scratch_shapes=[pltpu.VMEM((width, rows * size), jnp.bfloat16)],
        compiler_params=pltpu.CompilerParams(vmem_limit_bytes=16 * MIB),
        name="regroup",
    )(a_vals)


def product_kernel(*refs):
    tables, spreads_hbm, mixed_hbm, local_hbm = (refs[i : i + 2] for i in range(0, 8, 2))
    ghost_ref, out_ref, spread_ref, mixed_ref, local_ref, placed, picked, terms, prod, sems = refs[8:18]
    sums = refs[18:]
    _, rows, width, double = mixed_ref.shape
    size = double // 2
    w = size // 2
    links = width // size
    slots = ghost_ref.shape[0]
    copies = []
    for n, (here, there) in enumerate(((local_hbm, local_ref), (mixed_hbm, mixed_ref), (spreads_hbm, spread_ref))):
        for o in range(2):
            copies.append(pltpu.make_async_copy(here[o], there.at[o], sems.at[2 * n + o]))
    for copy in copies:
        copy.start()
    for total in sums:
        total[...] = jnp.zeros_like(total)
    row = lax.broadcasted_iota(jnp.int32, (width, width), 0)
    col = lax.broadcasted_iota(jnp.int32, (width, width), 1)
    near_link = (links * (row & (size - 1)) + row // size) // size
    keep = one_hot(col // size == near_link)
    for o in range(2):
        copies[o].wait()
        for r in range(rows):
            q = o * rows + r
            for a in range(links):
                if a == 0:
                    source = local_ref[o, r]
                else:
                    e = tables[o][a, PICKS * rows + r]
                    near = local_ref[o, jnp.minimum(e, rows - 1)]
                    far = ghost_ref[jnp.clip(e - rows, 0, slots - 1)]
                    source = jnp.where(e < rows, near, far)
                for k in range(PICKS):
                    h, l = divmod(k, 2)
                    picked[q, k * w : (k + 1) * w, a * size : (a + 1) * size] = source[
                        h * w : (h + 1) * w, l * size : (l + 1) * size
                    ]
    for o in range(2):
        copies[2 + o].wait()
        for r in range(rows):
            q = o * rows + r
            twice = mixed_ref[o, r]
            for t in range(0, width, double):
                stop = min(t + double, width)
                placed[q, :, t:stop] = twice[:, : stop - t] * keep[:, t:stop]
            terms[q] = lax.dot_general(picked[q], placed[q], NT, preferred_element_type=jnp.float32)
    for b in range(links):
        for k in range(PICKS):
            for odd in range(2):
                for u in range(rows):
                    o, r = divmod(2 * u + odd, rows)
                    here = pl.ds(pl.multiple_of(tables[o][b, rows * k + r], w), w)
                    lanes = slice(odd * size, (odd + 1) * size)
                    sums[u][here, lanes] = (
                        sums[u][here, lanes] + terms[2 * u + odd, k * w : (k + 1) * w, b * size : (b + 1) * size]
                    )
    for u in range(rows):
        prod[:, u * double : (u + 1) * double] = sums[u][...].astype(jnp.bfloat16)
    for copy in copies[4:]:
        copy.wait()
    whole = rows * size
    out_ref[...] = (
        lax.dot_general(spread_ref[0], prod[:, :whole], NT, preferred_element_type=jnp.float32)
        + lax.dot_general(spread_ref[1], prod[:, whole:], NT, preferred_element_type=jnp.float32)
    ).astype(jnp.bfloat16)


def product(mine, other, ghosts):
    _, spread, mixed, local = mine
    rows, width, double = mixed.shape
    size = double // 2
    wide = (NC + EXT) * (size // 2)
    operands = [mine[0], other[0]]
    for n in (1, 2, 3):
        operands += [in_hbm(mine[n]), in_hbm(other[n])]
    return pl.pallas_call(
        product_kernel,
        out_shape=jax.ShapeDtypeStruct((NC * size, wide), jnp.bfloat16),
        in_specs=[SMEM] * 2 + [HBM] * 6 + [VMEM],
        out_specs=VMEM,
        scratch_shapes=[
            pltpu.VMEM((2, *spread.shape), jnp.bfloat16),
            pltpu.VMEM((2, *mixed.shape), jnp.bfloat16),
            pltpu.VMEM((2, *local.shape), jnp.bfloat16),
            pltpu.VMEM((2 * rows, width, width), jnp.bfloat16),
            pltpu.VMEM((2 * rows, 2 * size, width), jnp.bfloat16),
            pltpu.VMEM((2 * rows, 2 * size, width), jnp.float32),
            pltpu.VMEM((wide, 2 * rows * size), jnp.bfloat16),
            pltpu.SemaphoreType.DMA((6,)),
        ]
        + [pltpu.VMEM((wide, double), jnp.float32)] * rows,
        compiler_params=pltpu.CompilerParams(vmem_limit_bytes=44 * MIB),
        name="product",
    )(*operands, ghosts)


def total_kernel(part_ref, out_ref):
    parts, size, wide = part_ref.shape
    halves = []
    for d in range(2):
        total = part_ref[d].astype(jnp.float32)
        for c in range(d + 2, parts, 2):
            total = total + part_ref[c].astype(jnp.float32)
        halves.append(total)
    group = 2 * size
    first = lax.broadcasted_iota(jnp.int32, (size, group), 1) // (size // 2) % 2 == 0
    for u in range(wide // group):
        low = halves[0][:, u * group : (u + 1) * group]
        high = halves[1][:, u * group : (u + 1) * group]
        out_ref[:, 0, 2 * u * group : (2 * u + 1) * group] = jnp.where(first, low, high)
        out_ref[:, 0, (2 * u + 1) * group : (2 * u + 2) * group] = jnp.where(
            first, pltpu.roll(low, group - size // 2, 1), pltpu.roll(high, size // 2, 1)
        )


def total(parts):
    _, size, wide = parts.shape
    return pl.pallas_call(
        total_kernel,
        out_shape=jax.ShapeDtypeStruct((size, 1, 2 * wide), jnp.float32),
        in_specs=[VMEM],
        out_specs=VMEM,
        compiler_params=pltpu.CompilerParams(vmem_limit_bytes=8 * MIB),
        name="total",
    )(parts)


def on_device(a_vals, a_cols, p_vals, p_cols, gp_cols, send_list):
    size = p_vals.shape[1]
    slots = send_list.shape[0]
    comp = lax.axis_size("comp")
    outgoing = pack(send_list, p_vals, comp)
    outgoing = outgoing.reshape(-1, *outgoing.shape[3:])
    arrived = lax.all_to_all(outgoing, ("fine", "inner", "comp"), split_axis=0, concat_axis=0, tiled=True)
    place = lax.axis_index("inner").reshape(1)
    columns = [jnp.pad(table.T, ((0, 0), (0, slots - table.shape[0]))) for table in (a_cols, p_cols, gp_cols)]
    swap = ((0, 1), (1, 0))
    a_other = lax.ppermute(a_vals, "inner", swap)
    table, table_sent = index(a_cols.shape[1], comp, place, jnp.concatenate(columns, axis=0))
    table_other = lax.ppermute(table_sent, "inner", swap)
    p_other = lax.ppermute(p_vals, "inner", swap)
    spread, local = layout(place, table, p_vals)
    mixed = regroup(a_vals)
    mixed_other = regroup(a_other)
    mixed_other, table_other, p_other = lax.optimization_barrier((mixed_other, table_other, p_other))
    spread_other, local_other = layout(place, table_other, p_other)
    partial = product((table, spread, mixed, local), (table_other, spread_other, mixed_other, local_other), arrived)
    moved = lax.all_to_all(partial, ("outer", "inner"), split_axis=0, concat_axis=0, tiled=True)
    owned = total(moved.reshape(NC, size, -1))
    return owned.reshape((1, owned.shape[0], 1, owned.shape[2]))


def solution(mesh):
    fine, coarse, comp = mesh.devices.shape
    pairs = Mesh(mesh.devices.reshape(fine, coarse // 2, 2, comp), ("fine", "outer", "inner", "comp"))
    rows = ("fine", "outer", "inner", "comp")
    placed = (
        P(rows, None, None),
        P(rows, None),
        P(rows, None, None),
        P(rows, None),
        P(rows, None),
        P(rows),
    )
    return jax.shard_map(
        on_device,
        mesh=pairs,
        in_specs=placed,
        out_specs=P("fine", ("outer", "inner"), "comp", None),
        check_vma=False,
    )
```

```python
import jax
import jax.numpy as jnp
from jax import lax
from jax.experimental import pallas as pl
from jax.experimental.pallas import tpu as pltpu
from jax.sharding import Mesh
from jax.sharding import PartitionSpec as P

NC = 8
EXT = 8
PICKS = 4

NT = (((1,), (1,)), ((), ()))
NN = (((1,), (0,)), ((), ()))
MIB = 1024 * 1024
VMEM = pl.BlockSpec(memory_space=pltpu.VMEM)
SMEM = pl.BlockSpec(memory_space=pltpu.SMEM)
HBM = pl.BlockSpec(memory_space=pltpu.HBM)


def in_hbm(array):
    return pltpu.with_memory_space_constraint(array, pltpu.HBM)


def one_hot(condition):
    return condition.astype(jnp.float32).astype(jnp.bfloat16)


def pack_kernel(send_hbm, p_hbm, sent_hbm, send_ref, p_ref, packed_ref, sems):
    rows, size, _ = p_ref.shape
    w = size // 2
    copies = [pltpu.make_async_copy(p_hbm, p_ref, sems.at[0]), pltpu.make_async_copy(send_hbm, send_ref, sems.at[1])]
    for copy in copies:
        copy.start()
    row = lax.broadcasted_iota(jnp.int32, (2 * size, PICKS * size), 0)
    col = lax.broadcasted_iota(jnp.int32, (2 * size, PICKS * size), 1)
    block = 2 * (row % size // w) * size + row // size * w + row % w
    lane = lax.broadcasted_iota(jnp.int32, (2 * size, 2 * size), 1)
    picks = [one_hot(col == block + l * size) for l in range(2)]
    for copy in copies:
        copy.wait()
    flat = p_ref[...].reshape(rows * size, PICKS * size)
    turned = [lax.dot_general(pick, flat, NT, preferred_element_type=jnp.float32) for pick in picks]
    for u in range(rows // 2):
        low = turned[0][:, u * 2 * size : (u + 1) * 2 * size]
        high = turned[1][:, u * 2 * size : (u + 1) * 2 * size]
        even = jnp.where(lane < size, low, pltpu.roll(high, size, 1)).astype(jnp.bfloat16)
        odd = jnp.where(lane < size, pltpu.roll(low, size, 1), high).astype(jnp.bfloat16)
        for d in range(2):
            packed_ref[2 * u, d] = even[d * size : (d + 1) * size]
            packed_ref[2 * u + 1, d] = odd[d * size : (d + 1) * size]
    moves = []
    for f in range(sent_hbm.shape[0]):
        for m in range(sent_hbm.shape[2]):
            slot = f * sent_hbm.shape[2] + m
            moves.append(pltpu.make_async_copy(packed_ref.at[send_ref[slot]], sent_hbm.at[f, :, m], sems.at[2]))
    for move in moves:
        move.start()
    pltpu.make_async_copy(sent_hbm, sent_hbm, sems.at[2]).wait()


def pack(send_list, p_vals, comp):
    rows, size, _ = p_vals.shape
    slots = send_list.shape[0]
    return pl.pallas_call(
        pack_kernel,
        out_shape=pltpu.HBM((slots // comp, 2, comp, size, 2 * size), p_vals.dtype),
        in_specs=[HBM, HBM],
        out_specs=HBM,
        scratch_shapes=[
            pltpu.SMEM((slots,), jnp.int32),
            pltpu.VMEM(p_vals.shape, p_vals.dtype),
            pltpu.VMEM((rows, 2, size, 2 * size), p_vals.dtype),
            pltpu.SemaphoreType.DMA((3,)),
        ],
        compiler_params=pltpu.CompilerParams(vmem_limit_bytes=8 * MIB),
        name="pack",
    )(in_hbm(send_list), in_hbm(p_vals))


def index_kernel(links, comp, place_ref, tables_ref, mine_ref, other_ref):
    rows = 3 * PICKS
    size = tables_ref.shape[1]
    w = size // 2
    place = place_ref[0]
    shift = comp.bit_length() - 1
    for b in range(links):
        for r in range(rows):
            e = tables_ref[b, r]
            is_local = e < rows
            near = jnp.minimum(e, rows - 1)
            far = jnp.clip(e - rows, 0, size - 1)
            slot = ((far >> shift) << (shift + 1)) + (place << shift) + (far & (comp - 1))
            source = jnp.where(is_local, near, rows + slot)
            mine_ref[b, PICKS * rows + r] = source
            other_ref[b, PICKS * rows + r] = source
            for k in range(PICKS):
                c = jnp.where(is_local, tables_ref[links + k, near], tables_ref[links + PICKS + k, far])
                base = (c & 12) + ((c & 1) << 1)
                upper = (c >> 1) & 1
                mine_ref[b, rows * k + r] = w * (base + (upper ^ place))
                other_ref[b, rows * k + r] = w * (base + (upper ^ place ^ 1))
    for k in range(PICKS):
        for r in range(rows):
            mine_ref[k, size + r] = tables_ref[links + k, r]
            other_ref[k, size + r] = tables_ref[links + k, r]


def index(links, comp, place, tables):
    assert comp & (comp - 1) == 0
    shape = jax.ShapeDtypeStruct((links, 2 * tables.shape[1]), jnp.int32)
    return pl.pallas_call(
        lambda *refs: index_kernel(links, comp, *refs),
        out_shape=[shape, shape],
        in_specs=[SMEM, SMEM],
        out_specs=[SMEM, SMEM],
        name="index",
    )(place, tables)


def lay_out(half, table_ref, p_ref, spread_ref, local_ref):
    rows, size, _ = p_ref.shape
    w = size // 2
    spread_ref[...] = jnp.zeros(spread_ref.shape, spread_ref.dtype)
    flat = p_ref[...].reshape(rows * size, PICKS * size)
    row = lax.broadcasted_iota(jnp.int32, (PICKS * size, PICKS * size), 0)
    col = lax.broadcasted_iota(jnp.int32, (PICKS * size, PICKS * size), 1)
    turned = lax.dot_general(one_hot(row == col), flat, NT, preferred_element_type=jnp.float32)
    for r in range(rows):
        for k in range(PICKS):
            start = pl.multiple_of(table_ref[k, size + r] * size, size)
            spread_ref[pl.ds(start, size), r * size : (r + 1) * size] = turned[
                k * size : (k + 1) * size, r * size : (r + 1) * size
            ].astype(jnp.bfloat16)
    row = lax.broadcasted_iota(jnp.int32, (size, PICKS * size), 0)
    col = lax.broadcasted_iota(jnp.int32, (size, PICKS * size), 1)
    block = 2 * size * jnp.where(row < w, 0, 1) + half * w + jnp.where(row < w, row, row - w)
    lane = lax.broadcasted_iota(jnp.int32, (size, 2 * size), 1)
    packed = [
        lax.dot_general(one_hot(col == block + l * size), flat, NT, preferred_element_type=jnp.float32) for l in range(2)
    ]
    for u in range(rows // 2):
        low = packed[0][:, u * 2 * size : (u + 1) * 2 * size]
        high = packed[1][:, u * 2 * size : (u + 1) * 2 * size]
        local_ref[2 * u] = jnp.where(lane < size, low, pltpu.roll(high, size, 1)).astype(jnp.bfloat16)
        local_ref[2 * u + 1] = jnp.where(lane < size, pltpu.roll(low, size, 1), high).astype(jnp.bfloat16)


def layout_kernel(half_ref, table_ref, p_ref, spread_ref, local_ref):
    lay_out(half_ref[0], table_ref, p_ref, spread_ref, local_ref)


def layout(half, table, p_vals):
    rows, size, _ = p_vals.shape
    return pl.pallas_call(
        layout_kernel,
        out_shape=[
            pltpu.HBM((NC * size, rows * size), p_vals.dtype),
            pltpu.HBM((rows, size, 2 * size), p_vals.dtype),
        ],
        in_specs=[SMEM, SMEM, VMEM],
        out_specs=[VMEM, VMEM],
        compiler_params=pltpu.CompilerParams(vmem_limit_bytes=12 * MIB),
        name="layout",
    )(half, table, p_vals)


def regroup_kernel(a_ref, mixed_ref, stacked):
    rows, size, width = a_ref.shape
    links = width // size
    row = lax.broadcasted_iota(jnp.int32, (width, width), 0)
    col = lax.broadcasted_iota(jnp.int32, (width, width), 1)
    pair = links * (row & (size - 1)) + row // size
    for r in range(rows):
        for a in range(links):
            stacked[a * size : (a + 1) * size, r * size : (r + 1) * size] = a_ref[r, :, a * size : (a + 1) * size]
    moved = lax.dot_general(one_hot(col == pair), stacked[...], NN, preferred_element_type=jnp.float32).astype(jnp.bfloat16)
    row = lax.broadcasted_iota(jnp.int32, (4 * size, 4 * size), 0)
    col = lax.broadcasted_iota(jnp.int32, (4 * size, 4 * size), 1)
    eye = one_hot(row == col)
    for r in range(0, rows, 4):
        turned = lax.dot_general(eye, moved[:, r * size : (r + 4) * size], NT, preferred_element_type=jnp.float32)
        for u in range(4):
            mixed_ref[r + u] = turned[u * size : (u + 1) * size].astype(jnp.bfloat16)


def regroup(a_vals):
    rows, size, width = a_vals.shape
    return pl.pallas_call(
        regroup_kernel,
        out_shape=pltpu.HBM((rows, size, width), a_vals.dtype),
        in_specs=[VMEM],
        out_specs=VMEM,
        scratch_shapes=[pltpu.VMEM((width, rows * size), jnp.bfloat16)],
        compiler_params=pltpu.CompilerParams(vmem_limit_bytes=16 * MIB),
        name="regroup",
    )(a_vals)


def product_kernel(*refs):
    half_ref, *tables, p_hbm, spread_hbm, local_hbm = refs[:6]
    mixed_hbm = refs[6:8]
    ghost_ref, out_ref, p_ref, spread_ref, mixed_ref, local_ref, placed, picked, terms, prod, sems = refs[8:19]
    sums = refs[19:]
    _, rows, size, width = mixed_ref.shape
    double = 2 * size
    w = size // 2
    links = width // size
    slots = ghost_ref.shape[0]
    copies = [
        pltpu.make_async_copy(here, there, sems.at[n])
        for n, (here, there) in enumerate(
            (
                (p_hbm, p_ref),
                (local_hbm, local_ref.at[0]),
                (mixed_hbm[0], mixed_ref.at[0]),
                (mixed_hbm[1], mixed_ref.at[1]),
                (spread_hbm, spread_ref.at[0]),
            )
        )
    ]
    for copy in copies:
        copy.start()
    for total in sums:
        total[...] = jnp.zeros_like(total)
    row = lax.broadcasted_iota(jnp.int32, (links + 1, width), 0)
    col = lax.broadcasted_iota(jnp.int32, (links + 1, width), 1)
    keep = one_hot(row == (links * (col & (size - 1)) + col // size) // size)
    copies[0].wait()
    lay_out(half_ref[0], tables[1], p_ref, spread_ref.at[1], local_ref.at[1])
    copies[1].wait()
    for o in range(2):
        for r in range(rows):
            q = o * rows + r
            for a in range(links):
                if a == 0:
                    source = local_ref[o, r]
                else:
                    e = tables[o][a, PICKS * rows + r]
                    near = local_ref[o, jnp.minimum(e, rows - 1)]
                    far = ghost_ref[jnp.clip(e - rows, 0, slots - 1)]
                    source = jnp.where(e < rows, near, far)
                for k in range(PICKS):
                    h, l = divmod(k, 2)
                    picked[q, k * w : (k + 1) * w, a * size : (a + 1) * size] = source[
                        h * w : (h + 1) * w, l * size : (l + 1) * size
                    ]
    def expand(q):
        o, r = divmod(q, rows)
        if r == 0:
            copies[2 + o].wait()
        part = mixed_ref[o, r]
        for a in range(links):
            placed[q % 4, a * size : (a + 1) * size, :] = part * keep[a : a + 1, :]

    expand(0)
    for q in range(2 * rows):
        if q + 1 < 2 * rows:
            expand(q + 1)
        terms[q] = lax.dot_general(picked[q], placed[q % 4], NN, preferred_element_type=jnp.float32)

        if q % 4 == 3:
            for b in range(links):
                for k in range(PICKS):
                    for odd in range(2):
                        for u in (q // 2 - 1, q // 2):
                            o, r = divmod(2 * u + odd, rows)
                            here = pl.ds(pl.multiple_of(tables[o][b, rows * k + r], w), w)
                            lanes = slice(odd * size, (odd + 1) * size)
                            sums[u][here, lanes] = (
                                sums[u][here, lanes] + terms[2 * u + odd, k * w : (k + 1) * w, b * size : (b + 1) * size]
                            )
    for u in range(rows):
        prod[:, u * double : (u + 1) * double] = sums[u][...].astype(jnp.bfloat16)
    copies[4].wait()
    whole = rows * size
    out_ref[...] = (
        lax.dot_general(spread_ref[0], prod[:, :whole], NT, preferred_element_type=jnp.float32)
        + lax.dot_general(spread_ref[1], prod[:, whole:], NT, preferred_element_type=jnp.float32)
    ).astype(jnp.bfloat16)


def product(half, tables, p_other, spread, local, mixed, ghosts):
    rows, size, width = mixed[0].shape
    wide = (NC + EXT) * (size // 2)
    operands = [in_hbm(array) for array in (p_other, spread, local, *mixed)]
    return pl.pallas_call(
        product_kernel,
        out_shape=jax.ShapeDtypeStruct((NC * size, wide), jnp.bfloat16),
        in_specs=[SMEM] * 3 + [HBM] * 5 + [VMEM],
        out_specs=VMEM,
        scratch_shapes=[
            pltpu.VMEM(p_other.shape, jnp.bfloat16),
            pltpu.VMEM((2, *spread.shape), jnp.bfloat16),
            pltpu.VMEM((2, *mixed[0].shape), jnp.bfloat16),
            pltpu.VMEM((2, *local.shape), jnp.bfloat16),
            pltpu.VMEM((4, width, width), jnp.bfloat16),
            pltpu.VMEM((2 * rows, 2 * size, width), jnp.bfloat16),
            pltpu.VMEM((2 * rows, 2 * size, width), jnp.float32),
            pltpu.VMEM((wide, 2 * rows * size), jnp.bfloat16),
            pltpu.SemaphoreType.DMA((5,)),
        ]
        + [pltpu.VMEM((wide, 2 * size), jnp.float32)] * rows,
        compiler_params=pltpu.CompilerParams(vmem_limit_bytes=40 * MIB),
        name="product",
    )(half, *tables, *operands, ghosts)


def total_kernel(part_ref, out_ref):
    parts, size, wide = part_ref.shape
    halves = []
    for d in range(2):
        total = part_ref[d].astype(jnp.float32)
        for c in range(d + 2, parts, 2):
            total = total + part_ref[c].astype(jnp.float32)
        halves.append(total)
    group = 2 * size
    first = lax.broadcasted_iota(jnp.int32, (size, group), 1) // (size // 2) % 2 == 0
    for u in range(wide // group):
        low = halves[0][:, u * group : (u + 1) * group]
        high = halves[1][:, u * group : (u + 1) * group]
        out_ref[:, 0, 2 * u * group : (2 * u + 1) * group] = jnp.where(first, low, high)
        out_ref[:, 0, (2 * u + 1) * group : (2 * u + 2) * group] = jnp.where(
            first, pltpu.roll(low, group - size // 2, 1), pltpu.roll(high, size // 2, 1)
        )


def total(parts):
    _, size, wide = parts.shape
    return pl.pallas_call(
        total_kernel,
        out_shape=jax.ShapeDtypeStruct((size, 1, 2 * wide), jnp.float32),
        in_specs=[VMEM],
        out_specs=VMEM,
        compiler_params=pltpu.CompilerParams(vmem_limit_bytes=8 * MIB),
        name="total",
    )(parts)


def on_device(a_vals, a_cols, p_vals, p_cols, gp_cols, send_list):
    size = p_vals.shape[1]
    slots = send_list.shape[0]
    comp = lax.axis_size("comp")
    outgoing = pack(send_list, p_vals, comp)
    outgoing = outgoing.reshape(-1, *outgoing.shape[3:])
    arrived = lax.all_to_all(outgoing, ("fine", "inner", "comp"), split_axis=0, concat_axis=0, tiled=True)
    place = lax.axis_index("inner").reshape(1)
    columns = [jnp.pad(table.T, ((0, 0), (0, slots - table.shape[0]))) for table in (a_cols, p_cols, gp_cols)]
    swap = ((0, 1), (1, 0))
    a_other = lax.ppermute(a_vals, "inner", swap)
    table, table_sent = index(a_cols.shape[1], comp, place, jnp.concatenate(columns, axis=0))
    table_other = lax.ppermute(table_sent, "inner", swap)
    p_other = lax.ppermute(p_vals, "inner", swap)
    spread, local = layout(place, table, p_vals)
    mixed = regroup(a_vals)
    mixed_other = regroup(a_other)
    mixed_other, table_other, p_other = lax.optimization_barrier((mixed_other, table_other, p_other))
    partial = product(place, (table, table_other), p_other, spread, local, (mixed, mixed_other), arrived)
    moved = lax.all_to_all(partial, ("outer", "inner"), split_axis=0, concat_axis=0, tiled=True)
    owned = total(moved.reshape(NC, size, -1))
    return owned.reshape((1, owned.shape[0], 1, owned.shape[2]))


def solution(mesh):
    fine, coarse, comp = mesh.devices.shape
    pairs = Mesh(mesh.devices.reshape(fine, coarse // 2, 2, comp), ("fine", "outer", "inner", "comp"))
    rows = ("fine", "outer", "inner", "comp")
    placed = (
        P(rows, None, None),
        P(rows, None),
        P(rows, None, None),
        P(rows, None),
        P(rows, None),
        P(rows),
    )
    return jax.shard_map(
        on_device,
        mesh=pairs,
        in_specs=placed,
        out_specs=P("fine", ("outer", "inner"), "comp", None),
        check_vma=False,
    )
```

```python
import jax
import jax.numpy as jnp
from jax import lax
from jax.experimental import pallas as pl
from jax.experimental.pallas import tpu as pltpu
from jax.sharding import Mesh
from jax.sharding import PartitionSpec as P

NC = 8
EXT = 8
PICKS = 4

NT = (((1,), (1,)), ((), ()))
NN = (((1,), (0,)), ((), ()))
MIB = 1024 * 1024
VMEM = pl.BlockSpec(memory_space=pltpu.VMEM)
SMEM = pl.BlockSpec(memory_space=pltpu.SMEM)
HBM = pl.BlockSpec(memory_space=pltpu.HBM)


def in_hbm(array):
    return pltpu.with_memory_space_constraint(array, pltpu.HBM)


def one_hot(condition):
    return condition.astype(jnp.float32).astype(jnp.bfloat16)


def pack_kernel(send_hbm, p_hbm, sent_hbm, send_ref, p_ref, packed_ref, sems):
    rows, size, _ = p_ref.shape
    w = size // 2
    copies = [pltpu.make_async_copy(p_hbm, p_ref, sems.at[0]), pltpu.make_async_copy(send_hbm, send_ref, sems.at[1])]
    for copy in copies:
        copy.start()
    row = lax.broadcasted_iota(jnp.int32, (2 * size, PICKS * size), 0)
    col = lax.broadcasted_iota(jnp.int32, (2 * size, PICKS * size), 1)
    block = 2 * (row % size // w) * size + row // size * w + row % w
    lane = lax.broadcasted_iota(jnp.int32, (2 * size, 2 * size), 1)
    picks = [one_hot(col == block + l * size) for l in range(2)]
    for copy in copies:
        copy.wait()
    flat = p_ref[...].reshape(rows * size, PICKS * size)
    turned = [lax.dot_general(pick, flat, NT, preferred_element_type=jnp.float32) for pick in picks]
    for u in range(rows // 2):
        low = turned[0][:, u * 2 * size : (u + 1) * 2 * size]
        high = turned[1][:, u * 2 * size : (u + 1) * 2 * size]
        even = jnp.where(lane < size, low, pltpu.roll(high, size, 1)).astype(jnp.bfloat16)
        odd = jnp.where(lane < size, pltpu.roll(low, size, 1), high).astype(jnp.bfloat16)
        for d in range(2):
            packed_ref[2 * u, d] = even[d * size : (d + 1) * size]
            packed_ref[2 * u + 1, d] = odd[d * size : (d + 1) * size]
    moves = []
    for f in range(sent_hbm.shape[0]):
        for m in range(sent_hbm.shape[2]):
            slot = f * sent_hbm.shape[2] + m
            moves.append(pltpu.make_async_copy(packed_ref.at[send_ref[slot]], sent_hbm.at[f, :, m], sems.at[2]))
    for move in moves:
        move.start()
    pltpu.make_async_copy(sent_hbm, sent_hbm, sems.at[2]).wait()


def pack(send_list, p_vals, comp):
    rows, size, _ = p_vals.shape
    slots = send_list.shape[0]
    return pl.pallas_call(
        pack_kernel,
        out_shape=pltpu.HBM((slots // comp, 2, comp, size, 2 * size), p_vals.dtype),
        in_specs=[HBM, HBM],
        out_specs=HBM,
        scratch_shapes=[
            pltpu.SMEM((slots,), jnp.int32),
            pltpu.VMEM(p_vals.shape, p_vals.dtype),
            pltpu.VMEM((rows, 2, size, 2 * size), p_vals.dtype),
            pltpu.SemaphoreType.DMA((3,)),
        ],
        compiler_params=pltpu.CompilerParams(vmem_limit_bytes=8 * MIB),
        name="pack",
    )(in_hbm(send_list), in_hbm(p_vals))


def index_kernel(links, comp, place_ref, tables_ref, mine_ref, other_ref):
    rows = 3 * PICKS
    size = tables_ref.shape[1]
    w = size // 2
    place = place_ref[0]
    shift = comp.bit_length() - 1
    for b in range(links):
        for r in range(rows):
            e = tables_ref[b, r]
            is_local = e < rows
            near = jnp.minimum(e, rows - 1)
            far = jnp.clip(e - rows, 0, size - 1)
            slot = ((far >> shift) << (shift + 1)) + (place << shift) + (far & (comp - 1))
            source = jnp.where(is_local, near, rows + slot)
            mine_ref[b, PICKS * rows + r] = source
            other_ref[b, PICKS * rows + r] = source
            for k in range(PICKS):
                c = jnp.where(is_local, tables_ref[links + k, near], tables_ref[links + PICKS + k, far])
                base = (c & 12) + ((c & 1) << 1)
                upper = (c >> 1) & 1
                mine_ref[b, rows * k + r] = w * (base + (upper ^ place))
                other_ref[b, rows * k + r] = w * (base + (upper ^ place ^ 1))
    for k in range(PICKS):
        for r in range(rows):
            mine_ref[k, size + r] = tables_ref[links + k, r]
            other_ref[k, size + r] = tables_ref[links + k, r]


def index(links, comp, place, tables):
    assert comp & (comp - 1) == 0
    shape = jax.ShapeDtypeStruct((links, 2 * tables.shape[1]), jnp.int32)
    return pl.pallas_call(
        lambda *refs: index_kernel(links, comp, *refs),
        out_shape=[shape, shape],
        in_specs=[SMEM, SMEM],
        out_specs=[SMEM, SMEM],
        name="index",
    )(place, tables)


def lay_out(half, table_ref, p_ref, spread_ref, local_ref):
    rows, size, _ = p_ref.shape
    w = size // 2
    spread_ref[...] = jnp.zeros(spread_ref.shape, spread_ref.dtype)
    flat = p_ref[...].reshape(rows * size, PICKS * size)
    row = lax.broadcasted_iota(jnp.int32, (PICKS * size, PICKS * size), 0)
    col = lax.broadcasted_iota(jnp.int32, (PICKS * size, PICKS * size), 1)
    turned = lax.dot_general(one_hot(row == col), flat, NT, preferred_element_type=jnp.float32)
    for r in range(rows):
        for k in range(PICKS):
            start = pl.multiple_of(table_ref[k, size + r] * size, size)
            spread_ref[pl.ds(start, size), r * size : (r + 1) * size] = turned[
                k * size : (k + 1) * size, r * size : (r + 1) * size
            ].astype(jnp.bfloat16)
    row = lax.broadcasted_iota(jnp.int32, (size, PICKS * size), 0)
    col = lax.broadcasted_iota(jnp.int32, (size, PICKS * size), 1)
    block = 2 * size * jnp.where(row < w, 0, 1) + half * w + jnp.where(row < w, row, row - w)
    lane = lax.broadcasted_iota(jnp.int32, (size, 2 * size), 1)
    packed = [
        lax.dot_general(one_hot(col == block + l * size), flat, NT, preferred_element_type=jnp.float32) for l in range(2)
    ]
    for u in range(rows // 2):
        low = packed[0][:, u * 2 * size : (u + 1) * 2 * size]
        high = packed[1][:, u * 2 * size : (u + 1) * 2 * size]
        local_ref[2 * u] = jnp.where(lane < size, low, pltpu.roll(high, size, 1)).astype(jnp.bfloat16)
        local_ref[2 * u + 1] = jnp.where(lane < size, pltpu.roll(low, size, 1), high).astype(jnp.bfloat16)


def layout_kernel(half_ref, table_ref, p_ref, spread_ref, local_ref):
    lay_out(half_ref[0], table_ref, p_ref, spread_ref, local_ref)


def layout(half, table, p_vals):
    rows, size, _ = p_vals.shape
    return pl.pallas_call(
        layout_kernel,
        out_shape=[
            pltpu.HBM((NC * size, rows * size), p_vals.dtype),
            pltpu.HBM((rows, size, 2 * size), p_vals.dtype),
        ],
        in_specs=[SMEM, SMEM, VMEM],
        out_specs=[VMEM, VMEM],
        compiler_params=pltpu.CompilerParams(vmem_limit_bytes=12 * MIB),
        name="layout",
    )(half, table, p_vals)


def regroup_kernel(a_ref, mixed_ref, stacked):
    rows, size, width = a_ref.shape
    links = width // size
    row = lax.broadcasted_iota(jnp.int32, (width, width), 0)
    col = lax.broadcasted_iota(jnp.int32, (width, width), 1)
    pair = links * (row & (size - 1)) + row // size
    for r in range(rows):
        for a in range(links):
            stacked[a * size : (a + 1) * size, r * size : (r + 1) * size] = a_ref[r, :, a * size : (a + 1) * size]
    moved = lax.dot_general(one_hot(col == pair), stacked[...], NN, preferred_element_type=jnp.float32).astype(jnp.bfloat16)
    row = lax.broadcasted_iota(jnp.int32, (4 * size, 4 * size), 0)
    col = lax.broadcasted_iota(jnp.int32, (4 * size, 4 * size), 1)
    eye = one_hot(row == col)
    for r in range(0, rows, 4):
        turned = lax.dot_general(eye, moved[:, r * size : (r + 4) * size], NT, preferred_element_type=jnp.float32)
        for u in range(4):
            mixed_ref[r + u] = turned[u * size : (u + 1) * size].astype(jnp.bfloat16)


def regroup(a_vals):
    rows, size, width = a_vals.shape
    return pl.pallas_call(
        regroup_kernel,
        out_shape=pltpu.HBM((rows, size, width), a_vals.dtype),
        in_specs=[VMEM],
        out_specs=VMEM,
        scratch_shapes=[pltpu.VMEM((width, rows * size), jnp.bfloat16)],
        compiler_params=pltpu.CompilerParams(vmem_limit_bytes=16 * MIB),
        name="regroup",
    )(a_vals)


def product_kernel(*refs):
    half_ref, *tables, p_hbm, spread_hbm, local_hbm = refs[:6]
    mixed_hbm = refs[6:8]
    ghost_ref, out_ref, p_ref, spread_ref, mixed_ref, local_ref, placed, picked, terms, prod, sems = refs[8:19]
    sums = refs[19:]
    _, rows, size, width = mixed_ref.shape
    double = 2 * size
    w = size // 2
    links = width // size
    slots = ghost_ref.shape[0]
    copies = [
        pltpu.make_async_copy(here, there, sems.at[n])
        for n, (here, there) in enumerate(
            (
                (p_hbm, p_ref),
                (local_hbm, local_ref.at[0]),
                (mixed_hbm[0], mixed_ref.at[0]),
                (mixed_hbm[1], mixed_ref.at[1]),
                (spread_hbm, spread_ref.at[0]),
            )
        )
    ]
    for copy in copies:
        copy.start()
    for total in sums:
        total[...] = jnp.zeros_like(total)
    row = lax.broadcasted_iota(jnp.int32, (links + 1, width), 0)
    col = lax.broadcasted_iota(jnp.int32, (links + 1, width), 1)
    keep = one_hot(row == (links * (col & (size - 1)) + col // size) // size)
    copies[0].wait()
    lay_out(half_ref[0], tables[1], p_ref, spread_ref.at[1], local_ref.at[1])
    copies[1].wait()
    lane = lax.broadcasted_iota(jnp.int32, (size, double), 1)

    def source(o, r, a):
        if a == 0:
            return local_ref[o, r]
        e = tables[o][a, PICKS * rows + r]
        near = local_ref[o, jnp.minimum(e, rows - 1)]
        far = ghost_ref[jnp.clip(e - rows, 0, slots - 1)]
        return jnp.where(e < rows, near, far)

    for o in range(2):
        for r in range(rows):
            q = o * rows + r
            for a in range(0, links, 2):
                low = source(o, r, a)
                if a + 1 < links:
                    high = source(o, r, a + 1)
                    blocks = [
                        jnp.where(lane < size, low, pltpu.roll(high, size, 1)),
                        jnp.where(lane < size, pltpu.roll(low, size, 1), high),
                    ]
                else:
                    blocks = [low[:, :size], low[:, size:]]
                for k in range(PICKS):
                    h, l = divmod(k, 2)
                    picked[q, k * w : (k + 1) * w, a * size : min(a + 2, links) * size] = blocks[l][h * w : (h + 1) * w]
    def expand(q):
        o, r = divmod(q, rows)
        if r == 0:
            copies[2 + o].wait()
        part = mixed_ref[o, r]
        for a in range(links):
            placed[q % 4, a * size : (a + 1) * size, :] = part * keep[a : a + 1, :]

    def add(pairs):
        for b in range(links):
            for k in range(PICKS):
                for odd in range(2):
                    for u in pairs:
                        o, r = divmod(2 * u + odd, rows)
                        here = pl.ds(pl.multiple_of(tables[o][b, rows * k + r], w), w)
                        lanes = slice(odd * size, (odd + 1) * size)
                        sums[u][here, lanes] = (
                            sums[u][here, lanes] + terms[2 * u + odd, k * w : (k + 1) * w, b * size : (b + 1) * size]
                        )
        for u in pairs:
            prod[:, u * double : (u + 1) * double] = sums[u][...].astype(jnp.bfloat16)

    whole = rows * size
    first = []

    def contract(o):
        return lax.dot_general(
            spread_ref[o], prod[:, o * whole : (o + 1) * whole], NT, preferred_element_type=jnp.float32
        )

    copies[4].wait()
    expand(0)
    for q in range(2 * rows):
        if q + 1 < 2 * rows:
            expand(q + 1)
        terms[q] = lax.dot_general(picked[q], placed[q % 4], NN, preferred_element_type=jnp.float32)
        if q % 4 == 3:
            u = q // 2 - 2
            if u >= 1:
                add((u - 1, u))
            if u == rows // 2 - 1:
                first.append(contract(0))
    add((rows - 2, rows - 1))
    out_ref[...] = (first[0] + contract(1)).astype(jnp.bfloat16)


def product(half, tables, p_other, spread, local, mixed, ghosts):
    rows, size, width = mixed[0].shape
    wide = (NC + EXT) * (size // 2)
    operands = [in_hbm(array) for array in (p_other, spread, local, *mixed)]
    return pl.pallas_call(
        product_kernel,
        out_shape=jax.ShapeDtypeStruct((NC * size, wide), jnp.bfloat16),
        in_specs=[SMEM] * 3 + [HBM] * 5 + [VMEM],
        out_specs=VMEM,
        scratch_shapes=[
            pltpu.VMEM(p_other.shape, jnp.bfloat16),
            pltpu.VMEM((2, *spread.shape), jnp.bfloat16),
            pltpu.VMEM((2, *mixed[0].shape), jnp.bfloat16),
            pltpu.VMEM((2, *local.shape), jnp.bfloat16),
            pltpu.VMEM((4, width, width), jnp.bfloat16),
            pltpu.VMEM((2 * rows, 2 * size, width), jnp.bfloat16),
            pltpu.VMEM((2 * rows, 2 * size, width), jnp.float32),
            pltpu.VMEM((wide, 2 * rows * size), jnp.bfloat16),
            pltpu.SemaphoreType.DMA((5,)),
        ]
        + [pltpu.VMEM((wide, 2 * size), jnp.float32)] * rows,
        compiler_params=pltpu.CompilerParams(vmem_limit_bytes=40 * MIB),
        name="product",
    )(half, *tables, *operands, ghosts)


def total_kernel(part_ref, out_ref):
    parts, size, wide = part_ref.shape
    halves = []
    for d in range(2):
        total = part_ref[d].astype(jnp.float32)
        for c in range(d + 2, parts, 2):
            total = total + part_ref[c].astype(jnp.float32)
        halves.append(total)
    group = 2 * size
    first = lax.broadcasted_iota(jnp.int32, (size, group), 1) // (size // 2) % 2 == 0
    for u in range(wide // group):
        low = halves[0][:, u * group : (u + 1) * group]
        high = halves[1][:, u * group : (u + 1) * group]
        out_ref[:, 0, 2 * u * group : (2 * u + 1) * group] = jnp.where(first, low, high)
        out_ref[:, 0, (2 * u + 1) * group : (2 * u + 2) * group] = jnp.where(
            first, pltpu.roll(low, group - size // 2, 1), pltpu.roll(high, size // 2, 1)
        )


def total(parts):
    _, size, wide = parts.shape
    return pl.pallas_call(
        total_kernel,
        out_shape=jax.ShapeDtypeStruct((size, 1, 2 * wide), jnp.float32),
        in_specs=[VMEM],
        out_specs=VMEM,
        compiler_params=pltpu.CompilerParams(vmem_limit_bytes=8 * MIB),
        name="total",
    )(parts)


def on_device(a_vals, a_cols, p_vals, p_cols, gp_cols, send_list):
    size = p_vals.shape[1]
    slots = send_list.shape[0]
    comp = lax.axis_size("comp")
    outgoing = pack(send_list, p_vals, comp)
    outgoing = outgoing.reshape(-1, *outgoing.shape[3:])
    arrived = lax.all_to_all(outgoing, ("fine", "inner", "comp"), split_axis=0, concat_axis=0, tiled=True)
    place = lax.axis_index("inner").reshape(1)
    columns = [jnp.pad(table.T, ((0, 0), (0, slots - table.shape[0]))) for table in (a_cols, p_cols, gp_cols)]
    swap = ((0, 1), (1, 0))
    a_other = lax.ppermute(a_vals, "inner", swap)
    table, table_sent = index(a_cols.shape[1], comp, place, jnp.concatenate(columns, axis=0))
    table_other = lax.ppermute(table_sent, "inner", swap)
    p_other = lax.ppermute(p_vals, "inner", swap)
    spread, local = layout(place, table, p_vals)
    mixed = regroup(a_vals)
    mixed_other = regroup(a_other)
    mixed_other, table_other, p_other = lax.optimization_barrier((mixed_other, table_other, p_other))
    partial = product(place, (table, table_other), p_other, spread, local, (mixed, mixed_other), arrived)
    moved = lax.all_to_all(partial, ("outer", "inner"), split_axis=0, concat_axis=0, tiled=True)
    owned = total(moved.reshape(NC, size, -1))
    return owned.reshape((1, owned.shape[0], 1, owned.shape[2]))


def solution(mesh):
    fine, coarse, comp = mesh.devices.shape
    pairs = Mesh(mesh.devices.reshape(fine, coarse // 2, 2, comp), ("fine", "outer", "inner", "comp"))
    rows = ("fine", "outer", "inner", "comp")
    placed = (
        P(rows, None, None),
        P(rows, None),
        P(rows, None, None),
        P(rows, None),
        P(rows, None),
        P(rows),
    )
    return jax.shard_map(
        on_device,
        mesh=pairs,
        in_specs=placed,
        out_specs=P("fine", ("outer", "inner"), "comp", None),
        check_vma=False,
    )
```

```python
import jax
import jax.numpy as jnp
from jax import lax
from jax.experimental import pallas as pl
from jax.experimental.pallas import tpu as pltpu
from jax.sharding import Mesh
from jax.sharding import PartitionSpec as P

NC = 8
EXT = 8
PICKS = 4

NT = (((1,), (1,)), ((), ()))
NN = (((1,), (0,)), ((), ()))
MIB = 1024 * 1024
VMEM = pl.BlockSpec(memory_space=pltpu.VMEM)
SMEM = pl.BlockSpec(memory_space=pltpu.SMEM)
HBM = pl.BlockSpec(memory_space=pltpu.HBM)


def in_hbm(array):
    return pltpu.with_memory_space_constraint(array, pltpu.HBM)


def one_hot(condition):
    return condition.astype(jnp.float32).astype(jnp.bfloat16)


def pack_kernel(send_hbm, p_hbm, sent_hbm, send_ref, p_ref, packed_ref, sems):
    rows, size, _ = p_ref.shape
    w = size // 2
    copies = [pltpu.make_async_copy(p_hbm, p_ref, sems.at[0]), pltpu.make_async_copy(send_hbm, send_ref, sems.at[1])]
    for copy in copies:
        copy.start()
    row = lax.broadcasted_iota(jnp.int32, (2 * size, PICKS * size), 0)
    col = lax.broadcasted_iota(jnp.int32, (2 * size, PICKS * size), 1)
    block = 2 * (row % size // w) * size + row // size * w + row % w
    lane = lax.broadcasted_iota(jnp.int32, (2 * size, 2 * size), 1)
    picks = [one_hot(col == block + l * size) for l in range(2)]
    for copy in copies:
        copy.wait()
    flat = p_ref[...].reshape(rows * size, PICKS * size)
    turned = [lax.dot_general(pick, flat, NT, preferred_element_type=jnp.float32) for pick in picks]
    for u in range(rows // 2):
        low = turned[0][:, u * 2 * size : (u + 1) * 2 * size]
        high = turned[1][:, u * 2 * size : (u + 1) * 2 * size]
        even = jnp.where(lane < size, low, pltpu.roll(high, size, 1)).astype(jnp.bfloat16)
        odd = jnp.where(lane < size, pltpu.roll(low, size, 1), high).astype(jnp.bfloat16)
        for d in range(2):
            packed_ref[2 * u, d] = even[d * size : (d + 1) * size]
            packed_ref[2 * u + 1, d] = odd[d * size : (d + 1) * size]
    moves = []
    for f in range(sent_hbm.shape[0]):
        for m in range(sent_hbm.shape[2]):
            slot = f * sent_hbm.shape[2] + m
            moves.append(pltpu.make_async_copy(packed_ref.at[send_ref[slot]], sent_hbm.at[f, :, m], sems.at[2]))
    for move in moves:
        move.start()
    pltpu.make_async_copy(sent_hbm, sent_hbm, sems.at[2]).wait()


def pack(send_list, p_vals, comp):
    rows, size, _ = p_vals.shape
    slots = send_list.shape[0]
    return pl.pallas_call(
        pack_kernel,
        out_shape=pltpu.HBM((slots // comp, 2, comp, size, 2 * size), p_vals.dtype),
        in_specs=[HBM, HBM],
        out_specs=HBM,
        scratch_shapes=[
            pltpu.SMEM((slots,), jnp.int32),
            pltpu.VMEM(p_vals.shape, p_vals.dtype),
            pltpu.VMEM((rows, 2, size, 2 * size), p_vals.dtype),
            pltpu.SemaphoreType.DMA((3,)),
        ],
        compiler_params=pltpu.CompilerParams(vmem_limit_bytes=8 * MIB),
        name="pack",
    )(in_hbm(send_list), in_hbm(p_vals))


def index_kernel(links, comp, place_ref, tables_ref, mine_ref, other_ref):
    rows = 3 * PICKS
    size = tables_ref.shape[1]
    w = size // 2
    place = place_ref[0]
    shift = comp.bit_length() - 1
    for b in range(links):
        for r in range(rows):
            e = tables_ref[b, r]
            is_local = e < rows
            near = jnp.minimum(e, rows - 1)
            far = jnp.clip(e - rows, 0, size - 1)
            slot = ((far >> shift) << (shift + 1)) + (place << shift) + (far & (comp - 1))
            source = jnp.where(is_local, near, rows + slot)
            mine_ref[b, PICKS * rows + r] = source
            other_ref[b, PICKS * rows + r] = source
            for k in range(PICKS):
                c = jnp.where(is_local, tables_ref[links + k, near], tables_ref[links + PICKS + k, far])
                base = (c & 12) + ((c & 1) << 1)
                upper = (c >> 1) & 1
                mine_ref[b, rows * k + r] = w * (base + (upper ^ place))
                other_ref[b, rows * k + r] = w * (base + (upper ^ place ^ 1))
    for k in range(PICKS):
        for r in range(rows):
            mine_ref[k, size + r] = tables_ref[links + k, r]
            other_ref[k, size + r] = tables_ref[links + k, r]


def index(links, comp, place, tables):
    assert comp & (comp - 1) == 0
    shape = jax.ShapeDtypeStruct((links, 2 * tables.shape[1]), jnp.int32)
    return pl.pallas_call(
        lambda *refs: index_kernel(links, comp, *refs),
        out_shape=[shape, shape],
        in_specs=[SMEM, SMEM],
        out_specs=[SMEM, SMEM],
        name="index",
    )(place, tables)


def lay_out(half, table_ref, p_ref, spread_ref, local_ref):
    rows, size, _ = p_ref.shape
    w = size // 2
    spread_ref[...] = jnp.zeros(spread_ref.shape, spread_ref.dtype)
    flat = p_ref[...].reshape(rows * size, PICKS * size)
    row = lax.broadcasted_iota(jnp.int32, (PICKS * size, PICKS * size), 0)
    col = lax.broadcasted_iota(jnp.int32, (PICKS * size, PICKS * size), 1)
    turned = lax.dot_general(one_hot(row == col), flat, NT, preferred_element_type=jnp.float32)
    for r in range(rows):
        for k in range(PICKS):
            start = pl.multiple_of(table_ref[k, size + r] * size, size)
            spread_ref[pl.ds(start, size), r * size : (r + 1) * size] = turned[
                k * size : (k + 1) * size, r * size : (r + 1) * size
            ].astype(jnp.bfloat16)
    row = lax.broadcasted_iota(jnp.int32, (size, PICKS * size), 0)
    col = lax.broadcasted_iota(jnp.int32, (size, PICKS * size), 1)
    block = 2 * size * jnp.where(row < w, 0, 1) + half * w + jnp.where(row < w, row, row - w)
    lane = lax.broadcasted_iota(jnp.int32, (size, 2 * size), 1)
    packed = [
        lax.dot_general(one_hot(col == block + l * size), flat, NT, preferred_element_type=jnp.float32) for l in range(2)
    ]
    for u in range(rows // 2):
        low = packed[0][:, u * 2 * size : (u + 1) * 2 * size]
        high = packed[1][:, u * 2 * size : (u + 1) * 2 * size]
        local_ref[2 * u] = jnp.where(lane < size, low, pltpu.roll(high, size, 1)).astype(jnp.bfloat16)
        local_ref[2 * u + 1] = jnp.where(lane < size, pltpu.roll(low, size, 1), high).astype(jnp.bfloat16)


def layout_kernel(half_ref, table_ref, p_ref, spread_ref, local_ref):
    lay_out(half_ref[0], table_ref, p_ref, spread_ref, local_ref)


def layout(half, table, p_vals):
    rows, size, _ = p_vals.shape
    return pl.pallas_call(
        layout_kernel,
        out_shape=[
            pltpu.HBM((NC * size, rows * size), p_vals.dtype),
            pltpu.HBM((rows, size, 2 * size), p_vals.dtype),
        ],
        in_specs=[SMEM, SMEM, VMEM],
        out_specs=[VMEM, VMEM],
        compiler_params=pltpu.CompilerParams(vmem_limit_bytes=12 * MIB),
        name="layout",
    )(half, table, p_vals)


def regroup_kernel(a_ref, mixed_ref, stacked):
    rows, size, width = a_ref.shape
    links = width // size
    row = lax.broadcasted_iota(jnp.int32, (width, width), 0)
    col = lax.broadcasted_iota(jnp.int32, (width, width), 1)
    pair = links * (row & (size - 1)) + row // size
    for r in range(rows):
        for a in range(links):
            stacked[a * size : (a + 1) * size, r * size : (r + 1) * size] = a_ref[r, :, a * size : (a + 1) * size]
    moved = lax.dot_general(one_hot(col == pair), stacked[...], NN, preferred_element_type=jnp.float32).astype(jnp.bfloat16)
    row = lax.broadcasted_iota(jnp.int32, (4 * size, 4 * size), 0)
    col = lax.broadcasted_iota(jnp.int32, (4 * size, 4 * size), 1)
    eye = one_hot(row == col)
    for r in range(0, rows, 4):
        turned = lax.dot_general(eye, moved[:, r * size : (r + 4) * size], NT, preferred_element_type=jnp.float32)
        for u in range(4):
            mixed_ref[r + u] = turned[u * size : (u + 1) * size].astype(jnp.bfloat16)


def regroup(a_vals):
    rows, size, width = a_vals.shape
    return pl.pallas_call(
        regroup_kernel,
        out_shape=pltpu.HBM((rows, size, width), a_vals.dtype),
        in_specs=[VMEM],
        out_specs=VMEM,
        scratch_shapes=[pltpu.VMEM((width, rows * size), jnp.bfloat16)],
        compiler_params=pltpu.CompilerParams(vmem_limit_bytes=16 * MIB),
        name="regroup",
    )(a_vals)


def product_kernel(*refs):
    half_ref, *tables, p_hbm, spread_hbm, local_hbm = refs[:6]
    mixed_hbm = refs[6:8]
    ghost_ref, out_ref, p_ref, spread_ref, mixed_ref, local_ref, placed, picked, terms, prod, sems = refs[8:19]
    sums = refs[19:]
    _, rows, size, width = mixed_ref.shape
    double = 2 * size
    w = size // 2
    links = width // size
    slots = ghost_ref.shape[0]
    copies = [
        pltpu.make_async_copy(here, there, sems.at[n])
        for n, (here, there) in enumerate(
            (
                (p_hbm, p_ref),
                (local_hbm, local_ref.at[0]),
                (mixed_hbm[0], mixed_ref.at[0]),
                (mixed_hbm[1], mixed_ref.at[1]),
                (spread_hbm, spread_ref.at[0]),
            )
        )
    ]
    for copy in copies:
        copy.start()
    for total in sums:
        total[...] = jnp.zeros_like(total)
    row = lax.broadcasted_iota(jnp.int32, (links + 1, width), 0)
    col = lax.broadcasted_iota(jnp.int32, (links + 1, width), 1)
    keep = one_hot(row == (links * (col & (size - 1)) + col // size) // size)
    copies[0].wait()
    lay_out(half_ref[0], tables[1], p_ref, spread_ref.at[1], local_ref.at[1])
    copies[1].wait()
    lane = lax.broadcasted_iota(jnp.int32, (size, double), 1)

    def source(o, r, a):
        if a == 0:
            return local_ref[o, r]
        e = tables[o][a, PICKS * rows + r]
        near = local_ref[o, jnp.minimum(e, rows - 1)]
        far = ghost_ref[jnp.clip(e - rows, 0, slots - 1)]
        return jnp.where(e < rows, near, far)

    for o in range(2):
        for r in range(rows):
            q = o * rows + r
            for a in range(0, links, 2):
                low = source(o, r, a)
                if a + 1 < links:
                    high = source(o, r, a + 1)
                    blocks = [
                        jnp.where(lane < size, low, pltpu.roll(high, size, 1)),
                        jnp.where(lane < size, pltpu.roll(low, size, 1), high),
                    ]
                else:
                    blocks = [low[:, :size], low[:, size:]]
                for k in range(PICKS):
                    h, l = divmod(k, 2)
                    picked[q, k * w : (k + 1) * w, a * size : min(a + 2, links) * size] = blocks[l][h * w : (h + 1) * w]
    def expand(q):
        o, r = divmod(q, rows)
        if r == 0:
            copies[2 + o].wait()
        part = mixed_ref[o, r]
        for a in range(links):
            placed[q % 4, a * size : (a + 1) * size, :] = part * keep[a : a + 1, :]

    def add(pairs):
        for b in range(links):
            for k in range(PICKS):
                for odd in range(2):
                    for u in pairs:
                        o, r = divmod(2 * u + odd, rows)
                        here = pl.ds(pl.multiple_of(tables[o][b, rows * k + r], w), w)
                        lanes = slice(odd * size, (odd + 1) * size)
                        sums[u][here, lanes] = (
                            sums[u][here, lanes] + terms[2 * u + odd, k * w : (k + 1) * w, b * size : (b + 1) * size]
                        )
        for u in pairs:
            prod[:, u * double : (u + 1) * double] = sums[u][...].astype(jnp.bfloat16)

    whole = rows * size
    first = []

    def contract(o):
        return lax.dot_general(
            spread_ref[o], prod[:, o * whole : (o + 1) * whole], NT, preferred_element_type=jnp.float32
        )

    copies[4].wait()
    expand(0)
    for q in range(2 * rows):
        if q + 1 < 2 * rows:
            expand(q + 1)
        terms[q] = lax.dot_general(picked[q], placed[q % 4], NN, preferred_element_type=jnp.float32)
        if q % 4 == 3:
            u = q // 2 - 2
            if u >= 1:
                add((u - 1, u))
            if u == rows // 2 - 1:
                first.append(contract(0))
    add((rows - 2, rows - 1))
    out_ref[...] = (first[0] + contract(1)).astype(jnp.bfloat16)


def product(half, tables, p_other, spread, local, mixed, ghosts):
    rows, size, width = mixed[0].shape
    wide = (NC + EXT) * (size // 2)
    operands = [in_hbm(array) for array in (p_other, spread, local, *mixed)]
    return pl.pallas_call(
        product_kernel,
        out_shape=jax.ShapeDtypeStruct((NC * size, wide), jnp.bfloat16),
        in_specs=[SMEM] * 3 + [HBM] * 5 + [VMEM],
        out_specs=VMEM,
        scratch_shapes=[
            pltpu.VMEM(p_other.shape, jnp.bfloat16),
            pltpu.VMEM((2, *spread.shape), jnp.bfloat16),
            pltpu.VMEM((2, *mixed[0].shape), jnp.bfloat16),
            pltpu.VMEM((2, *local.shape), jnp.bfloat16),
            pltpu.VMEM((4, width, width), jnp.bfloat16),
            pltpu.VMEM((2 * rows, 2 * size, width), jnp.bfloat16),
            pltpu.VMEM((2 * rows, 2 * size, width), jnp.float32),
            pltpu.VMEM((wide, 2 * rows * size), jnp.bfloat16),
            pltpu.SemaphoreType.DMA((5,)),
        ]
        + [pltpu.VMEM((wide, 2 * size), jnp.float32)] * rows,
        compiler_params=pltpu.CompilerParams(vmem_limit_bytes=40 * MIB),
        name="product",
    )(half, *tables, *operands, ghosts)


def total_kernel(part_ref, out_ref):
    parts, size, wide = part_ref.shape
    halves = []
    for d in range(2):
        total = part_ref[d].astype(jnp.float32)
        for c in range(d + 2, parts, 2):
            total = total + part_ref[c].astype(jnp.float32)
        halves.append(total)
    group = 2 * size
    first = lax.broadcasted_iota(jnp.int32, (size, group), 1) // (size // 2) % 2 == 0
    for u in range(wide // group):
        low = halves[0][:, u * group : (u + 1) * group]
        high = halves[1][:, u * group : (u + 1) * group]
        out_ref[:, 0, 2 * u * group : (2 * u + 1) * group] = jnp.where(first, low, high)
        out_ref[:, 0, (2 * u + 1) * group : (2 * u + 2) * group] = jnp.where(
            first, pltpu.roll(low, group - size // 2, 1), pltpu.roll(high, size // 2, 1)
        )


def total(parts):
    _, size, wide = parts.shape
    return pl.pallas_call(
        total_kernel,
        out_shape=jax.ShapeDtypeStruct((size, 1, 2 * wide), jnp.float32),
        in_specs=[VMEM],
        out_specs=VMEM,
        compiler_params=pltpu.CompilerParams(vmem_limit_bytes=8 * MIB),
        name="total",
    )(parts)


def on_device(a_vals, a_cols, p_vals, p_cols, gp_cols, send_list):
    size = p_vals.shape[1]
    slots = send_list.shape[0]
    comp = lax.axis_size("comp")
    outgoing = pack(send_list, p_vals, comp)
    outgoing = outgoing.reshape(-1, *outgoing.shape[3:])
    arrived = lax.all_to_all(outgoing, ("fine", "inner", "comp"), split_axis=0, concat_axis=0, tiled=True)
    place = lax.axis_index("inner").reshape(1)
    columns = [jnp.pad(table.T, ((0, 0), (0, slots - table.shape[0]))) for table in (a_cols, p_cols, gp_cols)]
    swap = ((0, 1), (1, 0))
    table, table_sent = index(a_cols.shape[1], comp, place, jnp.concatenate(columns, axis=0))
    table_other = lax.ppermute(table_sent, "inner", swap)
    p_sent, a_sent, table = lax.optimization_barrier((p_vals, a_vals, table))
    a_other = lax.ppermute(a_sent, "inner", swap)
    p_other = lax.ppermute(p_sent, "inner", swap)
    spread, local = layout(place, table, p_vals)
    mixed = regroup(a_vals)
    mixed_other = regroup(a_other)
    mixed_other, table_other, p_other = lax.optimization_barrier((mixed_other, table_other, p_other))
    partial = product(place, (table, table_other), p_other, spread, local, (mixed, mixed_other), arrived)
    moved = lax.all_to_all(partial, ("outer", "inner"), split_axis=0, concat_axis=0, tiled=True)
    owned = total(moved.reshape(NC, size, -1))
    return owned.reshape((1, owned.shape[0], 1, owned.shape[2]))


def solution(mesh):
    fine, coarse, comp = mesh.devices.shape
    pairs = Mesh(mesh.devices.reshape(fine, coarse // 2, 2, comp), ("fine", "outer", "inner", "comp"))
    rows = ("fine", "outer", "inner", "comp")
    placed = (
        P(rows, None, None),
        P(rows, None),
        P(rows, None, None),
        P(rows, None),
        P(rows, None),
        P(rows),
    )
    return jax.shard_map(
        on_device,
        mesh=pairs,
        in_specs=placed,
        out_specs=P("fine", ("outer", "inner"), "comp", None),
        check_vma=False,
    )
```
